256 devices in a mesh: chan: 8 (over y, core), dm: 8 (over z), bin: 4 (over x).
Axes of the slice: x: 4, y: 4, z: 8, core: 2. Of those that a mesh axis runs over, the one named last changes fastest.
Arguments:
- spectra: bfloat16 [2, 4, 8192, 4096], P(None, None, ('chan', 'dm'), 'bin'), may hold values from -6 to 6
- delays: int32 [8192, 64], P(('chan', 'dm')), may hold values from 0 to 8191
- templates: bfloat16 [2, 64, 64], replicated, may hold values from -0.5 to 0.5
Outputs:
- power: bfloat16 [64, 64, 4, 4096], P(('chan', 'dm'), None, None, 'bin')
The draws below stay inside these ranges and needn't reach their ends.
All inputs are finite; a program needn't handle non-finite values.
Results may differ from the reference program's by a relative error of at most 0.01.
Values may be sent and summed in bfloat16 or wider, within the bound.
No kernel may reach another device: no remote copies, remote signals or barrier semaphores. Data moves between devices by JAX's collectives and lax.ppermute only.
A program may use at most 64 MiB of HBM per device.

```python
import jax
import jax.numpy as jnp
from jax import lax

BEAMS = 4
D = 64
TEMPLATES = 64
TAPS = 64
K = 4096
C = 8192


def touch_ends(result, key, low, high):
    shape = result.shape
    spot = [jax.random.randint(jax.random.fold_in(key, axis), (), 0, shape[axis]) for axis in range(len(shape))]
    result = result.at[tuple(spot)].set(low)
    longest = shape.index(max(shape))
    spot[longest] = (spot[longest] + 1) % shape[longest]
    return result.at[tuple(spot)].set(high)


def steps_of(rng, shape, shards, least, high):
    level, own = 1.0, jax.random.fold_in(rng, 6)
    for dim, parts in shards:
        draws = jnp.exp(jax.random.uniform(jax.random.fold_in(own, dim), (parts,), jnp.float32, least / len(shards), high / len(shards)))
        level = level * jnp.repeat(draws, shape[dim] // parts).reshape([-1 if axis == dim else 1 for axis in range(len(shape))])
    return level


def normal_values(key, shape, width, bound, cuts=(), kind=jnp.bfloat16):
    drawn = jax.random.normal(key, shape, jnp.float32) * width
    if len(cuts) > 0:
        drawn = steps_of(key, shape, cuts, -0.22, 0.18) * drawn
    return jnp.clip(drawn, min=-bound, max=bound).astype(kind)


def setup_inputs(seed: int = 0) -> dict:
    keys = jax.random.split(jax.random.key(seed), 4)
    spectra = normal_values(keys[0], (2, BEAMS, C, K), 1.0, 6.0, ((2, 64), (3, 4)))
    delays = touch_ends(jax.random.randint(keys[1], (C, D), 0, 2 * K), jax.random.fold_in(keys[1], 1), 0, (2 * K) - 1).astype(jnp.int32)
    templates = normal_values(keys[2], (2, TEMPLATES, TAPS), (2 * TAPS) ** -0.5, 0.5)
    return {"spectra": spectra, "delays": delays, "templates": templates}


def reference(spectra, delays, templates):
    period = 2 * K
    norm_scale = 1.0 / (C ** 0.5)
    block_width = 32

    def one_block(position):
        offset = position * block_width
        bins = offset + jnp.arange(block_width, dtype=jnp.int32)
        product = (delays[:, :, None] * bins[None, None, :]) % period
        theta = product.astype(jnp.float32) * (jnp.pi / K)
        phase_re = lax.optimization_barrier(jnp.cos(theta).astype(jnp.bfloat16)).astype(jnp.float32)
        phase_im = lax.optimization_barrier((-jnp.sin(theta)).astype(jnp.bfloat16)).astype(jnp.float32)
        piece = lax.dynamic_slice_in_dim(spectra, offset, block_width, 3).astype(jnp.float32)
        real_sum = jnp.einsum("bck,cdk->dbk", piece[0], phase_re) - jnp.einsum("bck,cdk->dbk", piece[1], phase_im)
        imag_sum = jnp.einsum("bck,cdk->dbk", piece[0], phase_im) + jnp.einsum("bck,cdk->dbk", piece[1], phase_re)
        return jnp.stack([real_sum, imag_sum], axis=1) * norm_scale

    blocks = lax.map(one_block, jnp.arange(K // block_width, dtype=jnp.int32))
    dedispersed = jnp.moveaxis(blocks, 0, 3).reshape(D, 2, BEAMS, K).astype(jnp.bfloat16)

    weight_real = jnp.stack([templates[0], -templates[1]], axis=1)
    weight_imag = jnp.stack([templates[1], templates[0]], axis=1)
    tap_weights = jnp.concatenate([weight_real, weight_imag], axis=0).astype(jnp.float32)
    padded = jnp.pad(dedispersed, ((0, 0), (0, 0), (0, 0), (TAPS // 2, TAPS // 2)))

    def one_measure(measure_row):
        windows = jnp.stack([measure_row[:, :, shift_by:shift_by + K] for shift_by in range(TAPS)], axis=1)
        response = jnp.einsum("oct,ctbk->obk", tap_weights, windows.astype(jnp.float32))
        real_part = response[:TEMPLATES]
        imag_part = response[TEMPLATES:]
        return (real_part * real_part + imag_part * imag_part).astype(jnp.bfloat16)

    return lax.map(one_measure, padded)
```

```python
import math
from functools import partial

import jax
import jax.numpy as jnp
from jax import lax
from jax.experimental import pallas as pl
from jax.experimental.pallas import tpu as pltpu
from jax.sharding import PartitionSpec as P

D = 64
BEAMS = 4
TEMPLATES = 64
TAPS = 64
GROUP = 16
TILE = 128
SUB = TILE // GROUP
LANES = 2 * BEAMS
PHASE_DT = jnp.bfloat16
F32 = jnp.float32
BF16 = jnp.bfloat16


def swap_blocks(tiles):
    tiles = list(tiles)
    lane = lax.broadcasted_iota(jnp.int32, tiles[0].shape, 1)
    for step in (4, 2, 1):
        upper = (lane // GROUP) & step != 0
        fresh = list(tiles)
        for low in range(SUB):
            if low & step == 0:
                high = low | step
                fresh[low] = jnp.where(upper, pltpu.roll(tiles[high], step * GROUP, 1), tiles[low])
                fresh[high] = jnp.where(
                    upper, tiles[high], pltpu.roll(tiles[low], TILE - step * GROUP, 1)
                )
        tiles = fresh
    return tiles


def unit(count, period):
    rest = count & (period - 1)
    rest = jnp.where(rest >= period // 2, rest - period, rest)
    angle = rest.astype(F32) * (2.0 * math.pi / period)
    return jnp.cos(angle), jnp.sin(angle)


def times(a, b):
    return a[0] * b[0] - a[1] * b[1], a[0] * b[1] + a[1] * b[0]


def channel_sums(first_ref, delay_ref, x_ref, out_ref, fine_ref, mid_ref, base_ref, w_ref, *, period):
    tile = pl.program_id(0)
    half = GROUP // 2

    @pl.when(tile == 0)
    def _():
        n = delay_ref[...].T
        one = unit(n, period)
        group = unit(n * GROUP, period)
        wide = unit(n * TILE, period)
        start = unit(n * first_ref[0], period)
        power = one
        for j in range(1, half + 1):
            fine_ref[0, j] = power[0].astype(PHASE_DT)
            fine_ref[1, j] = power[1].astype(PHASE_DT)
            if j == half:
                mid = power
            power = times(power, one)
        for g in range(SUB):
            mid_ref[0, g] = mid[0]
            mid_ref[1, g] = mid[1]
            mid = times(mid, group)
        base_ref[0] = start[0]
        base_ref[1] = start[1]
        base_ref[2] = wide[0]
        base_ref[3] = wide[1]

    @pl.when(tile > 0)
    def _():
        moved = times((base_ref[0], base_ref[1]), (base_ref[2], base_ref[3]))
        base_ref[0] = moved[0]
        base_ref[1] = moved[1]

    lanes = lax.broadcasted_iota(jnp.int32, (128, TILE), 1)
    native = [x_ref[j // BEAMS, j % BEAMS].astype(F32) for j in range(LANES)]
    for g, mixed in enumerate(swap_blocks(native)):
        w_ref[g, 0:128, :] = mixed.astype(BF16)
        turned = pltpu.roll(mixed, TILE // 2, 1)
        w_ref[g, 128:256, :] = jnp.where(lanes >= TILE // 2, -turned, turned).astype(BF16)

    bin_of_lane = lax.broadcasted_iota(jnp.int32, (D, TILE), 1) & (GROUP - 1)

    def one_group(g):
        turn = times((base_ref[0], base_ref[1]), (mid_ref[0, g], mid_ref[1, g]))
        fc = turn[0].astype(PHASE_DT)
        fs = turn[1].astype(PHASE_DT)
        rows = [None] * GROUP
        rows[half] = (fc, fs)
        for j in range(1, half + 1):
            ec = fine_ref[0, j]
            es = fine_ref[1, j]
            cc = fc * ec
            ss = fs * es
            sc = fs * ec
            cs = fc * es
            if j < half:
                rows[half + j] = (cc - ss, sc + cs)
            rows[half - j] = (cc + ss, sc - cs)
        left = jnp.concatenate(
            [jnp.concatenate([c.astype(BF16), s.astype(BF16)], axis=1) for c, s in rows], axis=0
        )
        prod = jnp.dot(left, w_ref[g], preferred_element_type=F32)
        acc = prod[0:D]
        for k in range(1, GROUP):
            acc = jnp.where(bin_of_lane == k, prod[k * D : (k + 1) * D], acc)
        return acc.reshape(D // 8, 8, TILE)

    for pair in range(SUB // 2):
        both = jnp.concatenate([one_group(2 * pair), one_group(2 * pair + 1)], axis=1)
        out_ref[:, pl.ds(pair * 16, 16), :] = both.astype(BF16)


def dedisperse(spectra, delays, first, period):
    width = spectra.shape[3]
    tiles = width // TILE
    rows = width // GROUP * 8
    return pl.pallas_call(
        partial(channel_sums, period=period),
        grid_spec=pltpu.PrefetchScalarGridSpec(
            num_scalar_prefetch=1,
            grid=(tiles,),
            in_specs=[
                pl.BlockSpec((128, D), lambda i, s: (0, 0)),
                pl.BlockSpec((2, BEAMS, 128, TILE), lambda i, s: (0, 0, 0, i)),
            ],
            out_specs=pl.BlockSpec((D // 8, SUB * 8, TILE), lambda i, s: (0, i, 0)),
            scratch_shapes=[
                pltpu.VMEM((2, GROUP // 2 + 1, D, 128), PHASE_DT),
                pltpu.VMEM((2, SUB, D, 128), F32),
                pltpu.VMEM((4, D, 128), F32),
                pltpu.VMEM((SUB, 256, TILE), BF16),
            ],
        ),
        out_shape=jax.ShapeDtypeStruct((D // 8, rows, TILE), BF16),
        name="channel_sums",
    )(first, delays, spectra)


def fold_kernel(x_ref, out_ref, sum_ref):
    total = x_ref[0].astype(F32)
    for i in range(1, x_ref.shape[0]):
        total = total + x_ref[i].astype(F32)
    sum_ref[...] = total
    for d in range(8):
        out_ref[d] = sum_ref[pl.ds(d, total.shape[0] // 8, stride=8), :].astype(BF16)


def fold(received):
    count, rows, lanes = received.shape
    return pl.pallas_call(
        fold_kernel,
        out_shape=jax.ShapeDtypeStruct((8, rows // 8, lanes), BF16),
        scratch_shapes=[pltpu.VMEM((rows, lanes), F32)],
        name="fold",
    )(received)


def finish_kernel(x_ref, out_ref, *, scale):
    total = x_ref[0].astype(F32)
    for i in range(1, x_ref.shape[0]):
        total = total + x_ref[i].astype(F32)
    out_ref[...] = (total * scale).astype(BF16)


def finish(received, scale):
    return pl.pallas_call(
        partial(finish_kernel, scale=scale),
        out_shape=jax.ShapeDtypeStruct(received.shape[1:], BF16),
        name="finish",
    )(received)


def response_kernel(y_ref, left_ref, right_ref, h_ref, out_ref, u_ref, win_ref, pow_ref):
    rows = y_ref.shape[0]
    edge = left_ref.shape[0]
    tiles = rows // SUB
    u_ref[...] = jnp.zeros(u_ref.shape, F32)
    u_ref[0:edge, :] = left_ref[...].astype(F32)
    u_ref[pl.ds(edge, rows), :] = y_ref[...].astype(F32)
    u_ref[pl.ds(edge + rows, edge), :] = right_ref[...].astype(F32)
    blocks = [u_ref[pl.ds(g, 16, stride=SUB), :] for g in range(SUB)]
    series = swap_blocks(blocks)
    for j in range(LANES):
        ri, beam = divmod(j, BEAMS)
        for m in range(tiles):
            wide = jnp.concatenate([series[j][m : m + 1], series[j][m + 1 : m + 2]], axis=1)
            wide = jnp.broadcast_to(wide, (TAPS, 2 * TILE))
            turned = pltpu.roll(wide, 2 * TILE - (TAPS - 1), 1, stride=1, stride_axis=0)
            win_ref[beam, pl.ds(ri * TAPS, TAPS), pl.ds(m * TILE, TILE)] = turned[:, :TILE].astype(BF16)
    row = lax.broadcasted_iota(jnp.int32, (TAPS, TAPS), 0)
    col = lax.broadcasted_iota(jnp.int32, (TAPS, TAPS), 1)
    flip = jnp.where(row + col == TAPS - 1, 1.0, 0.0).astype(BF16)
    h_re = jnp.dot(h_ref[0], flip, preferred_element_type=F32)
    h_im = jnp.dot(h_ref[1], flip, preferred_element_type=F32)
    weights = jnp.concatenate(
        [jnp.concatenate([h_re, -h_im], axis=1), jnp.concatenate([h_im, h_re], axis=1)], axis=0
    ).astype(BF16)
    for beam in range(BEAMS):
        resp = jnp.dot(weights, win_ref[beam], preferred_element_type=F32)
        re = resp[:TEMPLATES]
        im = resp[TEMPLATES:]
        power = re * re + im * im
        for m in range(tiles):
            pow_ref[pl.ds(m * TEMPLATES * BEAMS + beam, TEMPLATES, stride=BEAMS), :] = power[:, m * TILE : (m + 1) * TILE]
    for m in range(tiles):
        part = pow_ref[pl.ds(m * TEMPLATES * BEAMS, TEMPLATES * BEAMS), :]
        out_ref[0, :, :, pl.ds(m * TILE, TILE)] = part.reshape(TEMPLATES, BEAMS, TILE).astype(BF16)


def response(y, left, right, templates):
    rows = y.shape[0]
    width = rows * GROUP
    return pl.pallas_call(
        response_kernel,
        out_shape=jax.ShapeDtypeStruct((1, TEMPLATES, BEAMS, width), BF16),
        scratch_shapes=[
            pltpu.VMEM((16 * SUB, TILE), F32),
            pltpu.VMEM((BEAMS, 2 * TAPS, width), BF16),
            pltpu.VMEM((TEMPLATES * BEAMS * width // TILE, TILE), F32),
        ],
        name="response",
    )(y, left, right, templates)


def shards(spectra, delays, templates):
    width = spectra.shape[3]
    period = 2 * width * lax.axis_size("bin")
    scale = 1.0 / math.sqrt(spectra.shape[2] * lax.axis_size(("chan", "dm")))
    first = (lax.axis_index("bin") * width).reshape(1).astype(jnp.int32)
    partial_sums = dedisperse(spectra, delays, first, period)
    received = lax.all_to_all(partial_sums, "chan", 0, 0, tiled=True)
    received = lax.all_to_all(fold(received), "dm", 0, 0, tiled=True)
    y = finish(received, scale)
    edge = TAPS // 2 // GROUP
    count = lax.axis_size("bin")
    up = [(i, i + 1) for i in range(count - 1)]
    down = [(i + 1, i) for i in range(count - 1)]
    left = lax.ppermute(y[y.shape[0] - edge :], "bin", up)
    right = lax.ppermute(y[:edge], "bin", down)
    return response(y, left, right, templates)


def solution(mesh):
    placed = (P(None, None, ("chan", "dm"), "bin"), P(("chan", "dm"), None), P())
    return jax.shard_map(
        shards,
        mesh=mesh,
        in_specs=placed,
        out_specs=P(("chan", "dm"), None, None, "bin"),
        check_vma=False,
    )
```

```python
import math
from functools import partial

import jax
import jax.numpy as jnp
from jax import lax
from jax.experimental import pallas as pl
from jax.experimental.pallas import tpu as pltpu
from jax.sharding import PartitionSpec as P

D = 64
BEAMS = 4
TEMPLATES = 64
TAPS = 64
GROUP = 16
TILE = 128
SUB = TILE // GROUP
LANES = 2 * BEAMS
PER_HOP = 16
PHASE_DT = jnp.bfloat16
F32 = jnp.float32
BF16 = jnp.bfloat16


def swap_blocks(tiles):
    tiles = list(tiles)
    lane = lax.broadcasted_iota(jnp.int32, tiles[0].shape, 1)
    for step in (4, 2, 1):
        upper = (lane // GROUP) & step != 0
        fresh = list(tiles)
        for low in range(SUB):
            if low & step == 0:
                high = low | step
                fresh[low] = jnp.where(upper, pltpu.roll(tiles[high], step * GROUP, 1), tiles[low])
                fresh[high] = jnp.where(
                    upper, tiles[high], pltpu.roll(tiles[low], TILE - step * GROUP, 1)
                )
        tiles = fresh
    return tiles


def unit(count, period):
    rest = count & (period - 1)
    rest = jnp.where(rest >= period // 2, rest - period, rest)
    angle = rest.astype(F32) * (2.0 * math.pi / period)
    return jnp.cos(angle), jnp.sin(angle)


def times(a, b):
    return a[0] * b[0] - a[1] * b[1], a[0] * b[1] + a[1] * b[0]


def near(x):
    return pltpu.with_memory_space_constraint(x, pltpu.VMEM)


def channel_sums(place_ref, delay_ref, x_ref, *rest, period, offsets, hops, build):
    out_refs, rest = rest[: len(offsets)], rest[len(offsets) :]
    if build:
        w_ref, fine_ref, mid_ref, base_ref = rest
    else:
        w_ref = x_ref
        fine_ref, mid_ref, base_ref = rest
    tile = pl.program_id(0)
    half = GROUP // 2
    count = len(offsets) * PER_HOP

    @pl.when(tile == 0)
    def _():
        n = jnp.concatenate(
            [
                delay_ref[pl.ds(pl.multiple_of((place_ref[1] + s) % hops * PER_HOP, PER_HOP), PER_HOP), :]
                for s in offsets
            ],
            axis=0,
        )
        one = unit(n, period)
        group = unit(n * GROUP, period)
        wide = unit(n * TILE, period)
        start = unit(n * place_ref[0], period)
        power = one
        for j in range(1, half + 1):
            fine_ref[0, j] = power[0].astype(PHASE_DT)
            fine_ref[1, j] = power[1].astype(PHASE_DT)
            if j == half:
                mid = power
            power = times(power, one)
        for g in range(SUB):
            mid_ref[0, g] = mid[0]
            mid_ref[1, g] = mid[1]
            mid = times(mid, group)
        base_ref[0] = start[0]
        base_ref[1] = start[1]
        base_ref[2] = wide[0]
        base_ref[3] = wide[1]

    @pl.when(tile > 0)
    def _():
        moved = times((base_ref[0], base_ref[1]), (base_ref[2], base_ref[3]))
        base_ref[0] = moved[0]
        base_ref[1] = moved[1]

    if build:
        lanes = lax.broadcasted_iota(jnp.int32, (128, TILE), 1)
        native = [x_ref[j // BEAMS, j % BEAMS].astype(F32) for j in range(LANES)]
        for g, mixed in enumerate(swap_blocks(native)):
            w_ref[tile * SUB + g, 0:128, :] = mixed.astype(BF16)
            turned = pltpu.roll(mixed, TILE // 2, 1)
            w_ref[tile * SUB + g, 128:256, :] = jnp.where(lanes >= TILE // 2, -turned, turned).astype(BF16)

    bin_of_lane = lax.broadcasted_iota(jnp.int32, (count, TILE), 1) & (GROUP - 1)

    def one_group(g):
        turn = times((base_ref[0], base_ref[1]), (mid_ref[0, g], mid_ref[1, g]))
        fc = turn[0].astype(PHASE_DT)
        fs = turn[1].astype(PHASE_DT)
        rows = [None] * GROUP
        rows[half] = (fc, fs)
        for j in range(1, half + 1):
            ec = fine_ref[0, j]
            es = fine_ref[1, j]
            cc = fc * ec
            ss = fs * es
            sc = fs * ec
            cs = fc * es
            if j < half:
                rows[half + j] = (cc - ss, sc + cs)
            rows[half - j] = (cc + ss, sc - cs)
        left = jnp.concatenate(
            [jnp.concatenate([c.astype(BF16), s.astype(BF16)], axis=1) for c, s in rows], axis=0
        )
        prod = jnp.dot(left, w_ref[tile * SUB + g], preferred_element_type=F32)
        acc = prod[0:count]
        for k in range(1, GROUP):
            acc = jnp.where(bin_of_lane == k, prod[k * count : (k + 1) * count], acc)
        return acc.reshape(count // 8, 8, TILE)

    for pair in range(SUB // 2):
        both = jnp.concatenate([one_group(2 * pair), one_group(2 * pair + 1)], axis=1)
        part = PER_HOP // 8
        for i, out_ref in enumerate(out_refs):
            out_ref[:, pl.ds(pl.multiple_of(tile * SUB * 8 + pair * 16, 16), 16), :] = both[i * part : (i + 1) * part].astype(out_ref.dtype)


def dedisperse(x, delays, place, period, offsets, hops, build, dtype):
    tiles = x.shape[3] // TILE if build else x.shape[0] // SUB
    count = len(offsets) * PER_HOP
    x_spec = pl.BlockSpec((2, BEAMS, 128, TILE), lambda i, s: (0, 0, 0, i))
    w_spec = pl.BlockSpec(memory_space=pltpu.VMEM)
    part = PER_HOP // 8
    out_specs = [pl.BlockSpec(memory_space=pltpu.VMEM)] * len(offsets)
    out_shapes = [pltpu.VMEM((part, tiles * SUB * 8, TILE), dtype)] * len(offsets)
    w_shape = pltpu.VMEM((tiles * SUB, 256, TILE), BF16)
    return pl.pallas_call(
        partial(channel_sums, period=period, offsets=offsets, hops=hops, build=build),
        grid_spec=pltpu.PrefetchScalarGridSpec(
            num_scalar_prefetch=1,
            grid=(tiles,),
            in_specs=[
                pl.BlockSpec((D, 128), lambda i, s: (0, 0)),
                x_spec if build else w_spec,
            ],
            out_specs=out_specs + [w_spec] * build,
            scratch_shapes=[
                pltpu.VMEM((2, GROUP // 2 + 1, count, 128), PHASE_DT),
                pltpu.VMEM((2, SUB, count, 128), F32),
                pltpu.VMEM((4, count, 128), F32),
            ],
        ),
        out_shape=out_shapes + [w_shape] * build,
        compiler_params=pltpu.CompilerParams(vmem_limit_bytes=24 * 2**20),
        name="channel_sums",
    )(place, delays, x if build else near(x))


def fold_kernel(own_ref, far_ref, up_ref, down_ref, out_ref, sum_ref):
    for core in range(own_ref.shape[0]):
        total = own_ref[core].astype(F32)
        for ref in (far_ref, up_ref, down_ref):
            total = total + ref[core].astype(F32)
        sum_ref[...] = total
        for d in range(8):
            out_ref[core * 8 + d] = sum_ref[pl.ds(d, total.shape[0] // 8, stride=8), :].astype(BF16)


def fold(own, far, up, down):
    cores, rows, lanes = own.shape
    return pl.pallas_call(
        fold_kernel,
        in_specs=[pl.BlockSpec(memory_space=pltpu.VMEM)] * 4,
        out_specs=pl.BlockSpec(memory_space=pltpu.VMEM),
        out_shape=pltpu.VMEM((cores * 8, rows // 8, lanes), BF16),
        scratch_shapes=[pltpu.VMEM((rows, lanes), F32)],
        compiler_params=pltpu.CompilerParams(vmem_limit_bytes=24 * 2**20),
        name="fold",
    )(near(own), near(far), near(up), near(down))


def finish_kernel(x_ref, out_ref, head_ref, tail_ref, *, scale):
    total = x_ref[0].astype(F32)
    for i in range(1, x_ref.shape[0]):
        total = total + x_ref[i].astype(F32)
    y = (total * scale).astype(BF16)
    edge = head_ref.shape[0]
    out_ref[...] = y
    head_ref[...] = y[:edge]
    tail_ref[...] = y[y.shape[0] - edge :]


def finish(received, scale, edge):
    rows, lanes = received.shape[1:]
    return pl.pallas_call(
        partial(finish_kernel, scale=scale),
        in_specs=[pl.BlockSpec(memory_space=pltpu.VMEM)] * 1,
        out_specs=[pl.BlockSpec(memory_space=pltpu.VMEM)] * 3,
        out_shape=[pltpu.VMEM((n, lanes), BF16) for n in (rows, edge, edge)],
        compiler_params=pltpu.CompilerParams(vmem_limit_bytes=24 * 2**20),
        name="finish",
    )(near(received))


def response_kernel(place_ref, y_ref, left_ref, right_ref, h_ref, out_ref, u_ref, win_ref, pow_ref):
    rows = y_ref.shape[0]
    edge = left_ref.shape[0]
    tiles = rows // SUB
    u_ref[...] = jnp.zeros(u_ref.shape, F32)
    u_ref[0:edge, :] = jnp.where(place_ref[0] > 0, left_ref[...].astype(F32), 0.0)
    u_ref[pl.ds(edge, rows), :] = y_ref[...].astype(F32)
    u_ref[pl.ds(edge + rows, edge), :] = jnp.where(place_ref[2] > 0, right_ref[...].astype(F32), 0.0)
    blocks = [u_ref[pl.ds(g, 16, stride=SUB), :] for g in range(SUB)]
    series = swap_blocks(blocks)
    for j in range(LANES):
        ri, beam = divmod(j, BEAMS)
        for m in range(tiles):
            wide = jnp.concatenate([series[j][m : m + 1], series[j][m + 1 : m + 2]], axis=1)
            wide = jnp.broadcast_to(wide, (TAPS, 2 * TILE))
            turned = pltpu.roll(wide, 2 * TILE - (TAPS - 1), 1, stride=1, stride_axis=0)
            win_ref[beam, pl.ds(ri * TAPS, TAPS), pl.ds(m * TILE, TILE)] = turned[:, :TILE].astype(BF16)
    row = lax.broadcasted_iota(jnp.int32, (TAPS, TAPS), 0)
    col = lax.broadcasted_iota(jnp.int32, (TAPS, TAPS), 1)
    flip = jnp.where(row + col == TAPS - 1, 1.0, 0.0).astype(BF16)
    h_re = jnp.dot(h_ref[0], flip, preferred_element_type=F32)
    h_im = jnp.dot(h_ref[1], flip, preferred_element_type=F32)
    weights = jnp.concatenate(
        [jnp.concatenate([h_re, -h_im], axis=1), jnp.concatenate([h_im, h_re], axis=1)], axis=0
    ).astype(BF16)
    for beam in range(BEAMS):
        resp = jnp.dot(weights, win_ref[beam], preferred_element_type=F32)
        re = resp[:TEMPLATES]
        im = resp[TEMPLATES:]
        power = re * re + im * im
        for m in range(tiles):
            pow_ref[pl.ds(m * TEMPLATES * BEAMS + beam, TEMPLATES, stride=BEAMS), :] = power[:, m * TILE : (m + 1) * TILE]
    for m in range(tiles):
        part = pow_ref[pl.ds(m * TEMPLATES * BEAMS, TEMPLATES * BEAMS), :]
        out_ref[0, :, :, pl.ds(m * TILE, TILE)] = part.reshape(TEMPLATES, BEAMS, TILE).astype(BF16)


def response(place, y, left, right, templates):
    rows = y.shape[0]
    width = rows * GROUP
    return pl.pallas_call(
        response_kernel,
        grid_spec=pltpu.PrefetchScalarGridSpec(
            num_scalar_prefetch=1,
            in_specs=[pl.BlockSpec(memory_space=pltpu.VMEM)] * 4,
            scratch_shapes=[
                pltpu.VMEM((16 * SUB, TILE), F32),
                pltpu.VMEM((BEAMS, 2 * TAPS, width), BF16),
                pltpu.VMEM((TEMPLATES * BEAMS * width // TILE, TILE), F32),
            ],
        ),
        out_shape=jax.ShapeDtypeStruct((1, TEMPLATES, BEAMS, width), BF16),
        compiler_params=pltpu.CompilerParams(vmem_limit_bytes=24 * 2**20),
        name="response",
    )(place, near(y), near(left), near(right), templates)


def shards(spectra, delays, templates):
    width = spectra.shape[3]
    bins = lax.axis_size("bin")
    chans = lax.axis_size("chan")
    dms = lax.axis_size("dm")
    period = 2 * width * bins
    scale = 1.0 / math.sqrt(spectra.shape[2] * chans * dms)
    cores = PER_HOP // 8
    hops = chans // cores
    place = jnp.stack(
        [
            lax.axis_index("bin") * width,
            lax.axis_index("chan") // cores,
            bins - 1 - lax.axis_index("bin"),
        ]
    ).astype(jnp.int32)
    table = delays.T

    def moved(x, s):
        return lax.ppermute(x, "chan", [(i, (i + s * cores) % chans) for i in range(chans)])

    far, weights = dedisperse(spectra, table, place, period, (2,), hops, True, BF16)
    far = moved(far, 2)
    up, down = dedisperse(weights, table, place, period, (1, 3), hops, False, BF16)
    up = moved(up, 1)
    down = moved(down, 3)
    (own,) = dedisperse(weights, table, place, period, (0,), hops, False, F32)
    groups = [
        [(hop * cores + core) * dms + dm for core in range(cores) for dm in range(dms)]
        for hop in range(hops)
    ]
    received = lax.all_to_all(
        fold(own, far, up, down), ("chan", "dm"), 0, 0, axis_index_groups=groups, tiled=True
    )
    edge = TAPS // 2 // GROUP
    y, head, tail = finish(received, scale, edge)
    left = lax.ppermute(tail, "bin", [(i, (i + 1) % bins) for i in range(bins)])
    right = lax.ppermute(head, "bin", [((i + 1) % bins, i) for i in range(bins)])
    return response(place, y, left, right, templates)


def solution(mesh):
    placed = (P(None, None, ("chan", "dm"), "bin"), P(("chan", "dm"), None), P())
    return jax.shard_map(
        shards,
        mesh=mesh,
        in_specs=placed,
        out_specs=P(("chan", "dm"), None, None, "bin"),
        check_vma=False,
    )
```

```python
import math
from functools import partial

import jax
import jax.numpy as jnp
from jax import lax
from jax.experimental import pallas as pl
from jax.experimental.pallas import tpu as pltpu
from jax.sharding import PartitionSpec as P

D = 64
BEAMS = 4
TEMPLATES = 64
TAPS = 64
GROUP = 16
TILE = 128
SUB = TILE // GROUP
LANES = 2 * BEAMS
PER_HOP = 16
STEPS = 2
PHASE_DT = jnp.bfloat16
F32 = jnp.float32
BF16 = jnp.bfloat16


def swap_blocks(tiles):
    tiles = list(tiles)
    lane = lax.broadcasted_iota(jnp.int32, tiles[0].shape, 1)
    for step in (4, 2, 1):
        upper = (lane // GROUP) & step != 0
        fresh = list(tiles)
        for low in range(SUB):
            if low & step == 0:
                high = low | step
                fresh[low] = jnp.where(upper, pltpu.roll(tiles[high], step * GROUP, 1), tiles[low])
                fresh[high] = jnp.where(
                    upper, tiles[high], pltpu.roll(tiles[low], TILE - step * GROUP, 1)
                )
        tiles = fresh
    return tiles


def unit(count, period):
    quarter = period // 4
    rest = (count & (period - 1)) + quarter // 2
    turns = rest // quarter
    x = ((rest & (quarter - 1)) - quarter // 2).astype(F32) * (2.0 * math.pi / period)
    z = x * x
    sine = x * (1.0 + z * (-1.0 / 6 + z * (1.0 / 120 + z * (-1.0 / 5040 + z * (1.0 / 362880)))))
    cosine = 1.0 + z * (-0.5 + z * (1.0 / 24 + z * (-1.0 / 720 + z * (1.0 / 40320))))
    odd = turns & 1 == 1
    first = jnp.where(odd, sine, cosine)
    second = jnp.where(odd, cosine, sine)
    return (
        jnp.where((turns + 1) & 2 == 2, -first, first),
        jnp.where(turns & 2 == 2, -second, second),
    )


def times(a, b):
    return a[0] * b[0] - a[1] * b[1], a[0] * b[1] + a[1] * b[0]


def near(x):
    return pltpu.with_memory_space_constraint(x, pltpu.VMEM)


def far_away(x):
    return pltpu.with_memory_space_constraint(x, pltpu.HBM)


def channel_sums(place_ref, delay_ref, x_ref, *rest, period, offsets, hops, build, per_step):
    outs = 2 if build else len(offsets)
    out_refs, rest = rest[:outs], rest[outs:]
    if build:
        w_ref, copy_ref, fine_ref, mid_ref, base_ref, native_ref, sems = rest

        def fetch(t):
            part = native_ref.shape[3] // STEPS
            span = pl.ds(pl.multiple_of(t * part, TILE), part)
            return pltpu.make_async_copy(x_ref.at[:, :, :, span], native_ref.at[:, :, :, span], sems.at[t])

    else:
        w_ref = x_ref
        fine_ref, mid_ref, base_ref = rest
    step = pl.program_id(0)
    half = GROUP // 2
    count = len(offsets) * PER_HOP

    @pl.when(step == 0)
    def _():
        if build:
            for t in range(STEPS):
                fetch(t).start()
            copy_ref[...] = delay_ref[...]
        n = jnp.concatenate(
            [
                delay_ref[pl.ds(pl.multiple_of((place_ref[1] + s) % hops * PER_HOP, PER_HOP), PER_HOP), :]
                for s in offsets
            ],
            axis=0,
        )
        one = unit(n, period)
        group = unit(n * GROUP, period)
        wide = unit(n * TILE, period)
        start = unit(n * place_ref[0], period)
        power = one
        for j in range(1, half + 1):
            fine_ref[0, j] = power[0].astype(PHASE_DT)
            fine_ref[1, j] = power[1].astype(PHASE_DT)
            if j == half:
                mid = power
            power = times(power, one)
        for g in range(SUB):
            mid_ref[0, g] = mid[0]
            mid_ref[1, g] = mid[1]
            mid = times(mid, group)
        base_ref[0] = start[0]
        base_ref[1] = start[1]
        base_ref[2] = wide[0]
        base_ref[3] = wide[1]

    if build:
        lanes = lax.broadcasted_iota(jnp.int32, (128, TILE), 1)
        fetch(step).wait()

    def build_weights(tile):
        span = pl.ds(pl.multiple_of(tile * TILE, TILE), TILE)
        native = [native_ref[j // BEAMS, j % BEAMS, :, span] for j in range(LANES)]
        for g, mixed in enumerate(swap_blocks(native)):
            at = tile * (SUB // 2) + g // 2
            side = pl.ds(g % 2 * TILE, TILE)
            w_ref[at, 0:128, side] = mixed
            turned = pltpu.roll(mixed, TILE // 2, 1)
            w_ref[at, 128:256, side] = jnp.where(lanes >= TILE // 2, -turned, turned)

    bin_of_lane = lax.broadcasted_iota(jnp.int32, (count, TILE), 1) & (GROUP - 1)

    def phases(base, g):
        turn = times(base, (mid_ref[0, g], mid_ref[1, g]))
        fc = turn[0].astype(PHASE_DT)
        fs = turn[1].astype(PHASE_DT)
        rows = [None] * GROUP
        rows[half] = (fc, fs)
        for j in range(1, half + 1):
            ec = fine_ref[0, j]
            es = fine_ref[1, j]
            cc = fc * ec
            ss = fs * es
            sc = fs * ec
            cs = fc * es
            if j < half:
                rows[half + j] = (cc - ss, sc + cs)
            rows[half - j] = (cc + ss, sc - cs)
        return [jnp.concatenate([c.astype(BF16), s.astype(BF16)], axis=1) for c, s in rows]

    def one_tile(tile, base):
        if build:
            build_weights(tile)
        for pair in range(SUB // 2):
            left = jnp.concatenate(phases(base, 2 * pair) + phases(base, 2 * pair + 1), axis=0)
            prod = jnp.dot(left, w_ref[tile * (SUB // 2) + pair], preferred_element_type=F32)
            sides = []
            for side in range(2):
                cols = slice(side * TILE, (side + 1) * TILE)
                first = side * GROUP * count
                acc = prod[first : first + count, cols]
                for k in range(1, GROUP):
                    row = first + k * count
                    acc = jnp.where(bin_of_lane == k, prod[row : row + count, cols], acc)
                sides.append(acc.reshape(count // 8, 8, TILE))
            both = jnp.concatenate(sides, axis=1)
            part = both.shape[0] // outs
            at = pl.ds(pl.multiple_of(tile * SUB * 8 + pair * 16, 16), 16)
            for i, out_ref in enumerate(out_refs):
                out_ref[:, at, :] = both[i * part : (i + 1) * part].astype(out_ref.dtype)

    base = (base_ref[0], base_ref[1])
    wide = (base_ref[2], base_ref[3])
    for sub in range(per_step):
        one_tile(step * per_step + sub, base)
        base = times(base, wide)
    base_ref[0] = base[0]
    base_ref[1] = base[1]


def dedisperse(x, delays, place, period, offsets, hops, build, dtype):
    tiles = x.shape[3] // TILE if build else x.shape[0] // (SUB // 2)
    count = len(offsets) * PER_HOP
    x_spec = pl.BlockSpec(memory_space=pl.ANY)
    stage = [pltpu.VMEM((2, BEAMS, 128, tiles * TILE), BF16), pltpu.SemaphoreType.DMA((STEPS,))]
    w_spec = pl.BlockSpec(memory_space=pltpu.VMEM)
    outs = 2 if build else len(offsets)
    part = count // 8 // outs
    out_specs = [pl.BlockSpec(memory_space=pltpu.VMEM)] * outs
    out_shapes = [pltpu.VMEM((part, tiles * SUB * 8, TILE), dtype)] * outs
    w_shape = pltpu.VMEM((tiles * SUB // 2, 256, 2 * TILE), BF16)
    return pl.pallas_call(
        partial(channel_sums, period=period, offsets=offsets, hops=hops, build=build, per_step=tiles // STEPS),
        grid_spec=pltpu.PrefetchScalarGridSpec(
            num_scalar_prefetch=1,
            grid=(STEPS,),
            in_specs=[
                pl.BlockSpec((D, 128), lambda i, s: (0, 0)) if build else w_spec,
                x_spec if build else w_spec,
            ],
            out_specs=out_specs + [w_spec, w_spec] * build,
            scratch_shapes=[
                pltpu.VMEM((2, GROUP // 2 + 1, count, 128), PHASE_DT),
                pltpu.VMEM((2, SUB, count, 128), F32),
                pltpu.VMEM((4, count, 128), F32),
            ]
            + stage * build,
        ),
        out_shape=out_shapes + [w_shape, pltpu.VMEM(delays.shape, delays.dtype)] * build,
        compiler_params=pltpu.CompilerParams(vmem_limit_bytes=24 * 2**20),
        name="channel_sums",
    )(place, far_away(delays) if build else near(delays), far_away(x) if build else near(x))


def fold_kernel(place_ref, own_ref, up_ref, down_ref, keep_ref, send_ref, sum_ref):
    core = place_ref[3]
    for which, out_ref in ((core, keep_ref), (1 - core, send_ref)):
        total = own_ref[which]
        for ref in (up_ref, down_ref):
            total = total + ref[which].astype(F32)
        sum_ref[...] = total
        for d in range(8):
            part = sum_ref[pl.ds(d, total.shape[0] // 8, stride=8), :]
            out_ref[d] = part.astype(out_ref.dtype)


def fold(place, own, up, down):
    _, rows, lanes = own.shape
    vmem = pl.BlockSpec(memory_space=pltpu.VMEM)
    return pl.pallas_call(
        fold_kernel,
        grid_spec=pltpu.PrefetchScalarGridSpec(
            num_scalar_prefetch=1,
            in_specs=[vmem] * 3,
            out_specs=[vmem] * 2,
            scratch_shapes=[pltpu.VMEM((rows, lanes), F32)],
        ),
        out_shape=[pltpu.VMEM((8, rows // 8, lanes), kind) for kind in (F32, BF16)],
        compiler_params=pltpu.CompilerParams(vmem_limit_bytes=24 * 2**20),
        name="fold",
    )(place, near(own), near(up), near(down))


def relay_kernel(up_ref, down_ref, first_ref, second_ref, up_out, down_out):
    for x_ref, far_ref, core, out_ref in ((up_ref, first_ref, 0, up_out), (down_ref, second_ref, 1, down_out)):
        out_ref[1 - core] = x_ref[1 - core].astype(BF16)
        out_ref[core] = (x_ref[core] + far_ref[0].astype(F32)).astype(BF16)


def relay(up, down, first, second):
    vmem = pl.BlockSpec(memory_space=pltpu.VMEM)
    return pl.pallas_call(
        relay_kernel,
        in_specs=[vmem] * 4,
        out_specs=[vmem] * 2,
        out_shape=[pltpu.VMEM(up.shape, BF16)] * 2,
        compiler_params=pltpu.CompilerParams(vmem_limit_bytes=24 * 2**20),
        name="relay",
    )(near(up), near(down), near(first), near(second))


def join_kernel(x_ref, y_ref, out_ref):
    out_ref[...] = (x_ref[...] + y_ref[...].astype(F32)).astype(BF16)


def join(kept, received):
    vmem = pl.BlockSpec(memory_space=pltpu.VMEM)
    return pl.pallas_call(
        join_kernel,
        in_specs=[vmem] * 2,
        out_specs=vmem,
        out_shape=pltpu.VMEM(kept.shape, BF16),
        compiler_params=pltpu.CompilerParams(vmem_limit_bytes=24 * 2**20),
        name="join",
    )(near(kept), near(received))


def finish_kernel(x_ref, out_ref, head_ref, tail_ref, *, scale):
    total = x_ref[0].astype(F32)
    for i in range(1, x_ref.shape[0]):
        total = total + x_ref[i].astype(F32)
    y = (total * scale).astype(BF16)
    edge = head_ref.shape[0]
    out_ref[...] = y
    head_ref[...] = y[:edge]
    tail_ref[...] = y[y.shape[0] - edge :]


def finish(received, scale, edge):
    rows, lanes = received.shape[1:]
    return pl.pallas_call(
        partial(finish_kernel, scale=scale),
        in_specs=[pl.BlockSpec(memory_space=pltpu.VMEM)] * 1,
        out_specs=[pl.BlockSpec(memory_space=pltpu.VMEM)] * 3,
        out_shape=[pltpu.VMEM((n, lanes), BF16) for n in (rows, edge, edge)],
        compiler_params=pltpu.CompilerParams(vmem_limit_bytes=24 * 2**20),
        name="finish",
    )(near(received))


def response_kernel(place_ref, y_ref, *rest, tiles, edges):
    if edges:
        left_ref, right_ref, h_ref, _, out_ref, u_ref, win_ref, pow_ref, part_ref, sems = rest
    else:
        h_ref, out_ref, u_ref, win_ref, pow_ref, part_ref, sems = rest
    rows = y_ref.shape[0]
    edge = TAPS // 2 // GROUP
    u_ref[...] = jnp.zeros(u_ref.shape, F32)
    u_ref[pl.ds(edge, rows), :] = y_ref[...].astype(F32)
    if edges:
        u_ref[0:edge, :] = jnp.where(place_ref[0] > 0, left_ref[...].astype(F32), 0.0)
        u_ref[pl.ds(edge + rows, edge), :] = jnp.where(place_ref[2] > 0, right_ref[...].astype(F32), 0.0)
    blocks = [u_ref[pl.ds(g, 16, stride=SUB), :] for g in range(SUB)]
    series = swap_blocks(blocks)
    for j in range(LANES):
        ri, beam = divmod(j, BEAMS)
        for i, m in enumerate(tiles):
            wide = jnp.concatenate([series[j][m : m + 1], series[j][m + 1 : m + 2]], axis=1)
            wide = jnp.broadcast_to(wide, (TAPS, 2 * TILE))
            turned = pltpu.roll(wide, 2 * TILE - (TAPS - 1), 1, stride=1, stride_axis=0)
            win_ref[beam, pl.ds(ri * TAPS, TAPS), pl.ds(i * TILE, TILE)] = turned[:, :TILE].astype(BF16)
    row = lax.broadcasted_iota(jnp.int32, (TAPS, TAPS), 0)
    col = lax.broadcasted_iota(jnp.int32, (TAPS, TAPS), 1)
    flip = jnp.where(row + col == TAPS - 1, 1.0, 0.0).astype(BF16)
    h_re = jnp.dot(h_ref[0], flip, preferred_element_type=F32)
    h_im = jnp.dot(h_ref[1], flip, preferred_element_type=F32)
    weights = jnp.concatenate(
        [jnp.concatenate([h_re, -h_im], axis=1), jnp.concatenate([h_im, h_re], axis=1)], axis=0
    ).astype(BF16)
    size = TEMPLATES * BEAMS
    for beam in range(BEAMS):
        resp = jnp.dot(weights, win_ref[beam], preferred_element_type=F32)
        re = resp[:TEMPLATES]
        im = resp[TEMPLATES:]
        power = re * re + im * im
        for i in range(len(tiles)):
            pow_ref[pl.ds(i * size + beam, TEMPLATES, stride=BEAMS), :] = power[:, i * TILE : (i + 1) * TILE]
    copies = []
    for i, m in enumerate(tiles):
        part = pow_ref[pl.ds(i * size, size), :]
        part_ref[i] = part.reshape(TEMPLATES, BEAMS, TILE).astype(BF16)
        copies.append(
            pltpu.make_async_copy(
                part_ref.at[i], out_ref.at[0, :, :, pl.ds(m * TILE, TILE)], sems.at[i]
            )
        )
        copies[-1].start()
    for copy in copies:
        copy.wait()


def response(place, y, templates, tiles, edges=(), before=()):
    width = y.shape[0] * GROUP
    count = len(tiles)
    vmem = pl.BlockSpec(memory_space=pltpu.VMEM)
    hbm = pl.BlockSpec(memory_space=pl.ANY)
    inputs = [near(y), *map(near, edges), templates]
    return pl.pallas_call(
        partial(response_kernel, tiles=tiles, edges=len(edges) > 0),
        grid_spec=pltpu.PrefetchScalarGridSpec(
            num_scalar_prefetch=1,
            in_specs=[vmem] * len(inputs) + [hbm] * len(before),
            out_specs=hbm,
            scratch_shapes=[
                pltpu.VMEM((16 * SUB, TILE), F32),
                pltpu.VMEM((BEAMS, 2 * TAPS, count * TILE), BF16),
                pltpu.VMEM((TEMPLATES * BEAMS * count, TILE), F32),
                pltpu.VMEM((count, TEMPLATES, BEAMS, TILE), BF16),
                pltpu.SemaphoreType.DMA((count,)),
            ],
        ),
        out_shape=jax.ShapeDtypeStruct((1, TEMPLATES, BEAMS, width), BF16),
        input_output_aliases={1 + len(inputs): 0} if before else {},
        compiler_params=pltpu.CompilerParams(vmem_limit_bytes=24 * 2**20),
        name="response",
    )(place, *inputs, *before)


def shards(spectra, delays, templates):
    width = spectra.shape[3]
    bins = lax.axis_size("bin")
    chans = lax.axis_size("chan")
    dms = lax.axis_size("dm")
    period = 2 * width * bins
    scale = 1.0 / math.sqrt(spectra.shape[2] * chans * dms)
    cores = PER_HOP // 8
    hops = chans // cores
    place = jnp.stack(
        [
            lax.axis_index("bin") * width,
            lax.axis_index("chan") // cores,
            bins - 1 - lax.axis_index("bin"),
            lax.axis_index("chan") % cores,
        ]
    ).astype(jnp.int32)
    table = delays.T

    def moved(x, s):
        return lax.ppermute(x, "chan", [(i, (i + s * cores) % chans) for i in range(chans)])

    first, second, weights, table = dedisperse(spectra, table, place, period, (2,), hops, True, BF16)
    first = moved(first, 1)
    second = moved(second, hops - 1)
    up, down = dedisperse(weights, table, place, period, (1, hops - 1), hops, False, F32)
    up, down = relay(up, down, first, second)
    up = moved(up, 1)
    down = moved(down, hops - 1)
    (own,) = dedisperse(weights, table, place, period, (0,), hops, False, F32)
    kept, sent = fold(place, own, up, down)
    other = lax.ppermute(
        sent, "chan", [(i, i // cores * cores + cores - 1 - i % cores) for i in range(chans)]
    )
    received = lax.all_to_all(join(kept, other), "dm", 0, 0, tiled=True)
    edge = TAPS // 2 // GROUP
    y, head, tail = finish(received, scale, edge)
    left = lax.ppermute(tail, "bin", [(i, (i + 1) % bins) for i in range(bins)])
    right = lax.ppermute(head, "bin", [((i + 1) % bins, i) for i in range(bins)])
    tiles = tuple(range(width // TILE))
    inner = response(place, y, templates, tiles[1:-1])
    return response(place, y, templates, (tiles[0], tiles[-1]), (left, right), (inner,))


def solution(mesh):
    placed = (P(None, None, ("chan", "dm"), "bin"), P(("chan", "dm"), None), P())
    return jax.shard_map(
        shards,
        mesh=mesh,
        in_specs=placed,
        out_specs=P(("chan", "dm"), None, None, "bin"),
        check_vma=False,
    )
```

```python
import math
from functools import partial

import jax
import jax.numpy as jnp
from jax import lax
from jax.experimental import pallas as pl
from jax.experimental.pallas import tpu as pltpu
from jax.sharding import PartitionSpec as P

D = 64
BEAMS = 4
TEMPLATES = 64
TAPS = 64
GROUP = 16
TILE = 128
SUB = TILE // GROUP
LANES = 2 * BEAMS
PER_HOP = 16
STEPS = 2
PIECES = 4
PHASE_DT = jnp.bfloat16
F32 = jnp.float32
BF16 = jnp.bfloat16


def swap_blocks(tiles):
    tiles = list(tiles)
    lane = lax.broadcasted_iota(jnp.int32, tiles[0].shape, 1)
    for step in (4, 2, 1):
        upper = (lane // GROUP) & step != 0
        fresh = list(tiles)
        for low in range(SUB):
            if low & step == 0:
                high = low | step
                fresh[low] = jnp.where(upper, pltpu.roll(tiles[high], step * GROUP, 1), tiles[low])
                fresh[high] = jnp.where(
                    upper, tiles[high], pltpu.roll(tiles[low], TILE - step * GROUP, 1)
                )
        tiles = fresh
    return tiles


def unit(count, period):
    quarter = period // 4
    rest = (count & (period - 1)) + quarter // 2
    turns = rest // quarter
    x = ((rest & (quarter - 1)) - quarter // 2).astype(F32) * (2.0 * math.pi / period)
    z = x * x
    sine = x * (1.0 + z * (-1.0 / 6 + z * (1.0 / 120 + z * (-1.0 / 5040 + z * (1.0 / 362880)))))
    cosine = 1.0 + z * (-0.5 + z * (1.0 / 24 + z * (-1.0 / 720 + z * (1.0 / 40320))))
    odd = turns & 1 == 1
    first = jnp.where(odd, sine, cosine)
    second = jnp.where(odd, cosine, sine)
    return (
        jnp.where((turns + 1) & 2 == 2, -first, first),
        jnp.where(turns & 2 == 2, -second, second),
    )


def times(a, b):
    return a[0] * b[0] - a[1] * b[1], a[0] * b[1] + a[1] * b[0]


def near(x):
    return pltpu.with_memory_space_constraint(x, pltpu.VMEM)


def far_away(x):
    return pltpu.with_memory_space_constraint(x, pltpu.HBM)


def channel_sums(place_ref, delay_ref, x_ref, *rest, period, hops, build, per_step):
    outs = 1
    out_refs, rest = rest[:outs], rest[outs:]
    if build:
        w_ref, copy_ref, fine_ref, mid_ref, base_ref, native_ref, sems = rest

        def fetch(t):
            part = native_ref.shape[3] // PIECES
            span = pl.ds(pl.multiple_of(t * part, TILE), part)
            return pltpu.make_async_copy(x_ref.at[:, :, :, span], native_ref.at[:, :, :, span], sems.at[t])

    else:
        w_ref = x_ref
        fine_ref, mid_ref, base_ref = rest
    step = pl.program_id(0)
    half = GROUP // 2
    count = hops * 8

    @pl.when(step == 0)
    def _():
        if build:
            for t in range(PIECES):
                fetch(t).start()
            copy_ref[...] = delay_ref[...]
        core = 1 - place_ref[3] if build else place_ref[3]
        first_rows = [(place_ref[1] + s) % hops * PER_HOP + core * 8 for s in range(hops)]
        n = jnp.concatenate([delay_ref[pl.ds(pl.multiple_of(r, 8), 8), :] for r in first_rows], axis=0)
        one = unit(n, period)
        group = unit(n * GROUP, period)
        wide = unit(n * TILE, period)
        start = unit(n * place_ref[0], period)
        power = one
        for j in range(1, half + 1):
            fine_ref[0, j] = power[0].astype(PHASE_DT)
            fine_ref[1, j] = power[1].astype(PHASE_DT)
            if j == half:
                mid = power
            power = times(power, one)
        for g in range(SUB):
            mid_ref[0, g] = mid[0]
            mid_ref[1, g] = mid[1]
            mid = times(mid, group)
        base_ref[0] = start[0]
        base_ref[1] = start[1]
        base_ref[2] = wide[0]
        base_ref[3] = wide[1]

    if build:
        lanes = lax.broadcasted_iota(jnp.int32, (128, TILE), 1)

    def build_weights(tile):
        span = pl.ds(pl.multiple_of(tile * TILE, TILE), TILE)
        native = [native_ref[j // BEAMS, j % BEAMS, :, span] for j in range(LANES)]
        for g, mixed in enumerate(swap_blocks(native)):
            at = tile * (SUB // 2) + g // 2
            w_ref[at, g % 2, 0:128] = mixed
            turned = pltpu.roll(mixed, TILE // 2, 1)
            w_ref[at, g % 2, 128:256] = jnp.where(lanes >= TILE // 2, -turned, turned)

    bin_of_lane = lax.broadcasted_iota(jnp.int32, (count, TILE), 1) & (GROUP - 1)

    def phases(base, g):
        turn = times(base, (mid_ref[0, g], mid_ref[1, g]))
        fc = turn[0].astype(PHASE_DT)
        fs = turn[1].astype(PHASE_DT)
        rows = [None] * GROUP
        rows[half] = (fc, fs)
        for j in range(1, half + 1):
            ec = fine_ref[0, j]
            es = fine_ref[1, j]
            cc = fc * ec
            ss = fs * es
            sc = fs * ec
            cs = fc * es
            if j < half:
                rows[half + j] = (cc - ss, sc + cs)
            rows[half - j] = (cc + ss, sc - cs)
        return [jnp.concatenate([c.astype(BF16), s.astype(BF16)], axis=1) for c, s in rows]

    def one_tile(tile, base):
        if build:
            build_weights(tile)
        for pair in range(SUB // 2):
            left = jnp.concatenate(phases(base, 2 * pair) + phases(base, 2 * pair + 1), axis=0)
            at = tile * (SUB // 2) + pair
            right = jnp.concatenate([w_ref[at, 0], w_ref[at, 1]], axis=1)
            prod = jnp.dot(left, right, preferred_element_type=F32)
            sides = []
            for side in range(2):
                cols = slice(side * TILE, (side + 1) * TILE)
                first = side * GROUP * count
                acc = prod[first : first + count, cols]
                for k in range(1, GROUP):
                    row = first + k * count
                    acc = jnp.where(bin_of_lane == k, prod[row : row + count, cols], acc)
                sides.append(acc.reshape(count // 8, 8, TILE))
            both = jnp.concatenate(sides, axis=1)
            part = both.shape[0] // outs
            at = pl.ds(pl.multiple_of(tile * SUB * 8 + pair * 16, 16), 16)
            for i, out_ref in enumerate(out_refs):
                out_ref[:, at, :] = both[i * part : (i + 1) * part].astype(out_ref.dtype)

    base = (base_ref[0], base_ref[1])
    wide = (base_ref[2], base_ref[3])
    per_piece = per_step * STEPS // PIECES
    for sub in range(per_step):
        if build and sub % per_piece == 0:
            fetch(step * (PIECES // STEPS) + sub // per_piece).wait()
        one_tile(step * per_step + sub, base)
        base = times(base, wide)
    base_ref[0] = base[0]
    base_ref[1] = base[1]


def dedisperse(x, delays, place, period, hops, build, dtype):
    tiles = x.shape[3] // TILE if build else x.shape[0] // (SUB // 2)
    count = hops * 8
    x_spec = pl.BlockSpec(memory_space=pl.ANY)
    stage = [pltpu.VMEM((2, BEAMS, 128, tiles * TILE), BF16), pltpu.SemaphoreType.DMA((PIECES,))]
    w_spec = pl.BlockSpec(memory_space=pltpu.VMEM)
    outs = 1
    part = count // 8 // outs
    out_specs = [pl.BlockSpec(memory_space=pltpu.VMEM)] * outs
    out_shapes = [pltpu.VMEM((part, tiles * SUB * 8, TILE), dtype)] * outs
    w_shape = pltpu.VMEM((tiles * SUB // 2, 2, 256, TILE), BF16)
    return pl.pallas_call(
        partial(channel_sums, period=period, hops=hops, build=build, per_step=tiles // STEPS),
        grid_spec=pltpu.PrefetchScalarGridSpec(
            num_scalar_prefetch=1,
            grid=(STEPS,),
            in_specs=[
                pl.BlockSpec((D, 128), lambda i, s: (0, 0)) if build else w_spec,
                x_spec if build else w_spec,
            ],
            out_specs=out_specs + [w_spec, w_spec] * build,
            scratch_shapes=[
                pltpu.VMEM((2, GROUP // 2 + 1, count, 128), PHASE_DT),
                pltpu.VMEM((2, SUB, count, 128), F32),
                pltpu.VMEM((4, count, 128), F32),
            ]
            + stage * build,
        ),
        out_shape=out_shapes + [w_shape, pltpu.VMEM(delays.shape, delays.dtype)] * build,
        compiler_params=pltpu.CompilerParams(vmem_limit_bytes=24 * 2**20),
        name="channel_sums",
    )(place, far_away(delays) if build else near(delays), far_away(x) if build else near(x))


def join_kernel(mine_ref, other_ref, keep_ref, *send_refs):
    keep_ref[...] = mine_ref[0] + other_ref[0].astype(F32)
    for s, send_ref in enumerate(send_refs, 1):
        send_ref[...] = (mine_ref[s] + other_ref[s].astype(F32)).astype(BF16)


def join(mine, other):
    vmem = pl.BlockSpec(memory_space=pltpu.VMEM)
    hops, rows, lanes = mine.shape
    return pl.pallas_call(
        join_kernel,
        in_specs=[vmem] * 2,
        out_specs=[vmem] * hops,
        out_shape=[pltpu.VMEM((rows, lanes), kind) for kind in [F32] + [BF16] * (hops - 1)],
        compiler_params=pltpu.CompilerParams(vmem_limit_bytes=24 * 2**20),
        name="join",
    )(near(mine), near(other))


def fold_kernel(keep_ref, *rest):
    *got_refs, out_ref, sum_ref = rest
    total = keep_ref[...]
    for ref in got_refs:
        total = total + ref[...].astype(F32)
    sum_ref[...] = total
    for d in range(8):
        out_ref[d] = sum_ref[pl.ds(d, total.shape[0] // 8, stride=8), :].astype(BF16)


def fold(kept, received):
    rows, lanes = kept.shape
    vmem = pl.BlockSpec(memory_space=pltpu.VMEM)
    return pl.pallas_call(
        fold_kernel,
        in_specs=[vmem] * (1 + len(received)),
        out_specs=vmem,
        out_shape=pltpu.VMEM((8, rows // 8, lanes), BF16),
        scratch_shapes=[pltpu.VMEM((rows, lanes), F32)],
        compiler_params=pltpu.CompilerParams(vmem_limit_bytes=24 * 2**20),
        name="fold",
    )(near(kept), *map(near, received))


def finish_kernel(x_ref, out_ref, head_ref, tail_ref, *, scale):
    total = x_ref[0].astype(F32)
    for i in range(1, x_ref.shape[0]):
        total = total + x_ref[i].astype(F32)
    y = (total * scale).astype(BF16)
    edge = head_ref.shape[0]
    out_ref[...] = y
    head_ref[...] = y[:edge]
    tail_ref[...] = y[y.shape[0] - edge :]


def finish(received, scale, edge):
    rows, lanes = received.shape[1:]
    return pl.pallas_call(
        partial(finish_kernel, scale=scale),
        in_specs=[pl.BlockSpec(memory_space=pltpu.VMEM)] * 1,
        out_specs=[pl.BlockSpec(memory_space=pltpu.VMEM)] * 3,
        out_shape=[pltpu.VMEM((n, lanes), BF16) for n in (rows, edge, edge)],
        compiler_params=pltpu.CompilerParams(vmem_limit_bytes=24 * 2**20),
        name="finish",
    )(near(received))


def response_kernel(place_ref, y_ref, *rest, tiles, edges):
    if edges:
        left_ref, right_ref, h_ref, _, out_ref, u_ref, win_ref, pow_ref, part_ref, sems = rest
    else:
        h_ref, out_ref, u_ref, win_ref, pow_ref, part_ref, sems = rest
    rows = y_ref.shape[0]
    edge = TAPS // 2 // GROUP
    u_ref[...] = jnp.zeros(u_ref.shape, F32)
    u_ref[pl.ds(edge, rows), :] = y_ref[...].astype(F32)
    if edges:
        u_ref[0:edge, :] = jnp.where(place_ref[0] > 0, left_ref[...].astype(F32), 0.0)
        u_ref[pl.ds(edge + rows, edge), :] = jnp.where(place_ref[2] > 0, right_ref[...].astype(F32), 0.0)
    blocks = [u_ref[pl.ds(g, 16, stride=SUB), :] for g in range(SUB)]
    series = swap_blocks(blocks)
    for j in range(LANES):
        ri, beam = divmod(j, BEAMS)
        for i, m in enumerate(tiles):
            wide = jnp.concatenate([series[j][m : m + 1], series[j][m + 1 : m + 2]], axis=1)
            wide = jnp.broadcast_to(wide, (TAPS, 2 * TILE))
            turned = pltpu.roll(wide, 2 * TILE - (TAPS - 1), 1, stride=1, stride_axis=0)
            win_ref[beam, pl.ds(ri * TAPS, TAPS), pl.ds(i * TILE, TILE)] = turned[:, :TILE].astype(BF16)
    row = lax.broadcasted_iota(jnp.int32, (TAPS, TAPS), 0)
    col = lax.broadcasted_iota(jnp.int32, (TAPS, TAPS), 1)
    flip = jnp.where(row + col == TAPS - 1, 1.0, 0.0).astype(BF16)
    h_re = jnp.dot(h_ref[0], flip, preferred_element_type=F32)
    h_im = jnp.dot(h_ref[1], flip, preferred_element_type=F32)
    weights = jnp.concatenate(
        [jnp.concatenate([h_re, -h_im], axis=1), jnp.concatenate([h_im, h_re], axis=1)], axis=0
    ).astype(BF16)
    size = TEMPLATES * BEAMS
    for beam in range(BEAMS):
        resp = jnp.dot(weights, win_ref[beam], preferred_element_type=F32)
        re = resp[:TEMPLATES]
        im = resp[TEMPLATES:]
        power = re * re + im * im
        for i in range(len(tiles)):
            pow_ref[pl.ds(i * size + beam, TEMPLATES, stride=BEAMS), :] = power[:, i * TILE : (i + 1) * TILE]
    copies = []
    for i, m in enumerate(tiles):
        part = pow_ref[pl.ds(i * size, size), :]
        part_ref[i] = part.reshape(TEMPLATES, BEAMS, TILE).astype(BF16)
        copies.append(
            pltpu.make_async_copy(
                part_ref.at[i], out_ref.at[0, :, :, pl.ds(m * TILE, TILE)], sems.at[i]
            )
        )
        copies[-1].start()
    for copy in copies:
        copy.wait()


def response(place, y, templates, tiles, edges=(), before=()):
    width = y.shape[0] * GROUP
    count = len(tiles)
    vmem = pl.BlockSpec(memory_space=pltpu.VMEM)
    hbm = pl.BlockSpec(memory_space=pl.ANY)
    inputs = [near(y), *map(near, edges), templates]
    return pl.pallas_call(
        partial(response_kernel, tiles=tiles, edges=len(edges) > 0),
        grid_spec=pltpu.PrefetchScalarGridSpec(
            num_scalar_prefetch=1,
            in_specs=[vmem] * len(inputs) + [hbm] * len(before),
            out_specs=hbm,
            scratch_shapes=[
                pltpu.VMEM((16 * SUB, TILE), F32),
                pltpu.VMEM((BEAMS, 2 * TAPS, count * TILE), BF16),
                pltpu.VMEM((TEMPLATES * BEAMS * count, TILE), F32),
                pltpu.VMEM((count, TEMPLATES, BEAMS, TILE), BF16),
                pltpu.SemaphoreType.DMA((count,)),
            ],
        ),
        out_shape=jax.ShapeDtypeStruct((1, TEMPLATES, BEAMS, width), BF16),
        input_output_aliases={1 + len(inputs): 0} if before else {},
        compiler_params=pltpu.CompilerParams(vmem_limit_bytes=24 * 2**20),
        name="response",
    )(place, *inputs, *before)


def shards(spectra, delays, templates):
    width = spectra.shape[3]
    bins = lax.axis_size("bin")
    chans = lax.axis_size("chan")
    dms = lax.axis_size("dm")
    period = 2 * width * bins
    scale = 1.0 / math.sqrt(spectra.shape[2] * chans * dms)
    cores = PER_HOP // 8
    hops = chans // cores
    place = jnp.stack(
        [
            lax.axis_index("bin") * width,
            lax.axis_index("chan") // cores,
            bins - 1 - lax.axis_index("bin"),
            lax.axis_index("chan") % cores,
        ]
    ).astype(jnp.int32)
    table = delays.T

    def moved(x, s):
        return lax.ppermute(x, "chan", [(i, (i + s * cores) % chans) for i in range(chans)])

    other, weights, table = dedisperse(spectra, table, place, period, hops, True, BF16)
    other = lax.ppermute(
        other, "chan", [(i, i // cores * cores + cores - 1 - i % cores) for i in range(chans)]
    )
    (mine,) = dedisperse(weights, table, place, period, hops, False, F32)
    kept, *sent = join(mine, other)
    order = sorted(range(1, hops), key=lambda s: -min(s, hops - s))
    received = [moved(sent[s - 1], s) for s in order]
    received = lax.all_to_all(fold(kept, received), "dm", 0, 0, tiled=True)
    edge = TAPS // 2 // GROUP
    y, head, tail = finish(received, scale, edge)
    left = lax.ppermute(tail, "bin", [(i, (i + 1) % bins) for i in range(bins)])
    right = lax.ppermute(head, "bin", [((i + 1) % bins, i) for i in range(bins)])
    tiles = tuple(range(width // TILE))
    inner = response(place, y, templates, tiles[1:-1])
    return response(place, y, templates, (tiles[0], tiles[-1]), (left, right), (inner,))


def solution(mesh):
    placed = (P(None, None, ("chan", "dm"), "bin"), P(("chan", "dm"), None), P())
    return jax.shard_map(
        shards,
        mesh=mesh,
        in_specs=placed,
        out_specs=P(("chan", "dm"), None, None, "bin"),
        check_vma=False,
    )
```

```python
import math
from functools import partial

import jax
import jax.numpy as jnp
from jax import lax
from jax.experimental import pallas as pl
from jax.experimental.pallas import tpu as pltpu
from jax.sharding import PartitionSpec as P

D = 64
BEAMS = 4
TEMPLATES = 64
TAPS = 64
GROUP = 16
TILE = 128
SUB = TILE // GROUP
LANES = 2 * BEAMS
PER_HOP = 16
STEPS = 1
PIECES = 1
PHASE_DT = jnp.bfloat16
F32 = jnp.float32
BF16 = jnp.bfloat16


def swap_blocks(tiles):
    tiles = list(tiles)
    lane = lax.broadcasted_iota(jnp.int32, tiles[0].shape, 1)
    for step in (4, 2, 1):
        upper = (lane // GROUP) & step != 0
        fresh = list(tiles)
        for low in range(SUB):
            if low & step == 0:
                high = low | step
                fresh[low] = jnp.where(upper, pltpu.roll(tiles[high], step * GROUP, 1), tiles[low])
                fresh[high] = jnp.where(
                    upper, tiles[high], pltpu.roll(tiles[low], TILE - step * GROUP, 1)
                )
        tiles = fresh
    return tiles


def unit(count, period):
    quarter = period // 4
    rest = (count & (period - 1)) + quarter // 2
    turns = rest // quarter
    x = ((rest & (quarter - 1)) - quarter // 2).astype(F32) * (2.0 * math.pi / period)
    z = x * x
    sine = x * (1.0 + z * (-1.0 / 6 + z * (1.0 / 120 + z * (-1.0 / 5040 + z * (1.0 / 362880)))))
    cosine = 1.0 + z * (-0.5 + z * (1.0 / 24 + z * (-1.0 / 720 + z * (1.0 / 40320))))
    odd = turns & 1 == 1
    first = jnp.where(odd, sine, cosine)
    second = jnp.where(odd, cosine, sine)
    return (
        jnp.where((turns + 1) & 2 == 2, -first, first),
        jnp.where(turns & 2 == 2, -second, second),
    )


def times(a, b):
    return a[0] * b[0] - a[1] * b[1], a[0] * b[1] + a[1] * b[0]


def near(x):
    return pltpu.with_memory_space_constraint(x, pltpu.VMEM)


def far_away(x):
    return pltpu.with_memory_space_constraint(x, pltpu.HBM)


def channel_sums(place_ref, delay_ref, x_ref, *rest, period, hops, build, per_step):
    outs = 1
    out_refs, rest = rest[:outs], rest[outs:]
    if build:
        w_ref, copy_ref, fine_ref, mid_ref, base_ref, native_ref, sems = rest

        def fetch(t):
            part = native_ref.shape[3] // PIECES
            span = pl.ds(pl.multiple_of(t * part, TILE), part)
            return pltpu.make_async_copy(x_ref.at[:, :, :, span], native_ref.at[:, :, :, span], sems.at[t])

    else:
        w_ref = x_ref
        fine_ref, mid_ref, base_ref = rest
    step = pl.program_id(0)
    half = GROUP // 2
    count = hops * 8

    @pl.when(step == 0)
    def _():
        if build:
            for t in range(PIECES):
                fetch(t).start()
            copy_ref[...] = delay_ref[...]
        core = 1 - place_ref[3] if build else place_ref[3]
        first_rows = [(place_ref[1] + s) % hops * PER_HOP + core * 8 for s in range(hops)]
        n = jnp.concatenate([delay_ref[pl.ds(pl.multiple_of(r, 8), 8), :] for r in first_rows], axis=0)
        one = unit(n, period)
        group = unit(n * GROUP, period)
        wide = unit(n * TILE, period)
        start = unit(n * place_ref[0], period)
        power = one
        for j in range(1, half + 1):
            fine_ref[0, j] = power[0].astype(PHASE_DT)
            fine_ref[1, j] = power[1].astype(PHASE_DT)
            if j == half:
                mid = power
            power = times(power, one)
        for g in range(SUB):
            mid_ref[0, g] = mid[0]
            mid_ref[1, g] = mid[1]
            mid = times(mid, group)
        base_ref[0] = start[0]
        base_ref[1] = start[1]
        base_ref[2] = wide[0]
        base_ref[3] = wide[1]

    if build:
        lanes = lax.broadcasted_iota(jnp.int32, (128, TILE), 1)

    def build_weights(tile):
        span = pl.ds(pl.multiple_of(tile * TILE, TILE), TILE)
        native = [native_ref[j // BEAMS, j % BEAMS, :, span] for j in range(LANES)]
        for g, mixed in enumerate(swap_blocks(native)):
            at = tile * (SUB // 2) + g // 2
            w_ref[at, g % 2, 0:128] = mixed
            turned = pltpu.roll(mixed, TILE // 2, 1)
            w_ref[at, g % 2, 128:256] = jnp.where(lanes >= TILE // 2, -turned, turned)

    bin_of_lane = lax.broadcasted_iota(jnp.int32, (count, TILE), 1) & (GROUP - 1)

    def phases(base, g):
        turn = times(base, (mid_ref[0, g], mid_ref[1, g]))
        fc = turn[0].astype(PHASE_DT)
        fs = turn[1].astype(PHASE_DT)
        rows = [None] * GROUP
        rows[half] = (fc, fs)
        for j in range(1, half + 1):
            ec = fine_ref[0, j]
            es = fine_ref[1, j]
            cc = fc * ec
            ss = fs * es
            sc = fs * ec
            cs = fc * es
            if j < half:
                rows[half + j] = (cc - ss, sc + cs)
            rows[half - j] = (cc + ss, sc - cs)
        return [jnp.concatenate([c.astype(BF16), s.astype(BF16)], axis=1) for c, s in rows]

    def one_tile(tile, base):
        if build:
            build_weights(tile)
        for pair in range(SUB // 2):
            left = jnp.concatenate(phases(base, 2 * pair) + phases(base, 2 * pair + 1), axis=0)
            at = tile * (SUB // 2) + pair
            right = jnp.concatenate([w_ref[at, 0], w_ref[at, 1]], axis=1)
            prod = jnp.dot(left, right, preferred_element_type=F32)
            sides = []
            for side in range(2):
                cols = slice(side * TILE, (side + 1) * TILE)
                first = side * GROUP * count
                acc = prod[first : first + count, cols]
                for k in range(1, GROUP):
                    row = first + k * count
                    acc = jnp.where(bin_of_lane == k, prod[row : row + count, cols], acc)
                sides.append(acc.reshape(count // 8, 8, TILE))
            both = jnp.concatenate(sides, axis=1)
            part = both.shape[0] // outs
            at = pl.ds(pl.multiple_of(tile * SUB * 8 + pair * 16, 16), 16)
            for i, out_ref in enumerate(out_refs):
                out_ref[:, at, :] = both[i * part : (i + 1) * part].astype(out_ref.dtype)

    base = (base_ref[0], base_ref[1])
    wide = (base_ref[2], base_ref[3])
    per_piece = per_step * STEPS // PIECES
    for sub in range(per_step):
        if build and sub % per_piece == 0:
            fetch(step * (PIECES // STEPS) + sub // per_piece).wait()
        one_tile(step * per_step + sub, base)
        base = times(base, wide)
    base_ref[0] = base[0]
    base_ref[1] = base[1]


def dedisperse(x, delays, place, period, hops, build, dtype):
    tiles = x.shape[3] // TILE if build else x.shape[0] // (SUB // 2)
    count = hops * 8
    x_spec = pl.BlockSpec(memory_space=pl.ANY)
    stage = [pltpu.VMEM((2, BEAMS, 128, tiles * TILE), BF16), pltpu.SemaphoreType.DMA((PIECES,))]
    w_spec = pl.BlockSpec(memory_space=pltpu.VMEM)
    outs = 1
    part = count // 8 // outs
    out_specs = [pl.BlockSpec(memory_space=pltpu.VMEM)] * outs
    out_shapes = [pltpu.VMEM((part, tiles * SUB * 8, TILE), dtype)] * outs
    w_shape = pltpu.VMEM((tiles * SUB // 2, 2, 256, TILE), BF16)
    return pl.pallas_call(
        partial(channel_sums, period=period, hops=hops, build=build, per_step=tiles // STEPS),
        grid_spec=pltpu.PrefetchScalarGridSpec(
            num_scalar_prefetch=1,
            grid=(STEPS,),
            in_specs=[
                pl.BlockSpec((D, 128), lambda i, s: (0, 0)) if build else w_spec,
                x_spec if build else w_spec,
            ],
            out_specs=out_specs + [w_spec, w_spec] * build,
            scratch_shapes=[
                pltpu.VMEM((2, GROUP // 2 + 1, count, 128), PHASE_DT),
                pltpu.VMEM((2, SUB, count, 128), F32),
                pltpu.VMEM((4, count, 128), F32),
            ]
            + stage * build,
        ),
        out_shape=out_shapes + [w_shape, pltpu.VMEM(delays.shape, delays.dtype)] * build,
        compiler_params=pltpu.CompilerParams(vmem_limit_bytes=24 * 2**20),
        name="channel_sums",
    )(place, far_away(delays) if build else near(delays), far_away(x) if build else near(x))


def join_kernel(mine_ref, other_ref, keep_ref, *send_refs):
    keep_ref[...] = mine_ref[0] + other_ref[0].astype(F32)
    for s, send_ref in enumerate(send_refs, 1):
        send_ref[...] = (mine_ref[s] + other_ref[s].astype(F32)).astype(BF16)


def join(mine, other):
    vmem = pl.BlockSpec(memory_space=pltpu.VMEM)
    hops, rows, lanes = mine.shape
    return pl.pallas_call(
        join_kernel,
        in_specs=[vmem] * 2,
        out_specs=[vmem] * hops,
        out_shape=[pltpu.VMEM((rows, lanes), kind) for kind in [F32] + [BF16] * (hops - 1)],
        compiler_params=pltpu.CompilerParams(vmem_limit_bytes=24 * 2**20),
        name="join",
    )(near(mine), near(other))


def fold_kernel(keep_ref, *rest):
    *got_refs, out_ref, sum_ref = rest
    total = keep_ref[...]
    for ref in got_refs:
        total = total + ref[...].astype(F32)
    sum_ref[...] = total
    for d in range(8):
        out_ref[d] = sum_ref[pl.ds(d, total.shape[0] // 8, stride=8), :].astype(BF16)


def fold(kept, received):
    rows, lanes = kept.shape
    vmem = pl.BlockSpec(memory_space=pltpu.VMEM)
    return pl.pallas_call(
        fold_kernel,
        in_specs=[vmem] * (1 + len(received)),
        out_specs=vmem,
        out_shape=pltpu.VMEM((8, rows // 8, lanes), BF16),
        scratch_shapes=[pltpu.VMEM((rows, lanes), F32)],
        compiler_params=pltpu.CompilerParams(vmem_limit_bytes=24 * 2**20),
        name="fold",
    )(near(kept), *map(near, received))


def finish_kernel(x_ref, out_ref, head_ref, tail_ref, *, scale):
    total = x_ref[0].astype(F32)
    for i in range(1, x_ref.shape[0]):
        total = total + x_ref[i].astype(F32)
    y = (total * scale).astype(BF16)
    edge = head_ref.shape[0]
    out_ref[...] = y
    head_ref[...] = y[:edge]
    tail_ref[...] = y[y.shape[0] - edge :]


def finish(received, scale, edge):
    rows, lanes = received.shape[1:]
    return pl.pallas_call(
        partial(finish_kernel, scale=scale),
        in_specs=[pl.BlockSpec(memory_space=pltpu.VMEM)] * 1,
        out_specs=[pl.BlockSpec(memory_space=pltpu.VMEM)] * 3,
        out_shape=[pltpu.VMEM((n, lanes), BF16) for n in (rows, edge, edge)],
        compiler_params=pltpu.CompilerParams(vmem_limit_bytes=24 * 2**20),
        name="finish",
    )(near(received))


def response_kernel(place_ref, y_ref, *rest, tiles, edges):
    if edges:
        left_ref, right_ref, h_ref, _, out_ref, u_ref, win_ref, pow_ref, part_ref, sems = rest
    else:
        h_ref, out_ref, u_ref, win_ref, pow_ref, part_ref, sems = rest
    rows = y_ref.shape[0]
    edge = TAPS // 2 // GROUP
    u_ref[...] = jnp.zeros(u_ref.shape, F32)
    u_ref[pl.ds(edge, rows), :] = y_ref[...].astype(F32)
    if edges:
        u_ref[0:edge, :] = jnp.where(place_ref[0] > 0, left_ref[...].astype(F32), 0.0)
        u_ref[pl.ds(edge + rows, edge), :] = jnp.where(place_ref[2] > 0, right_ref[...].astype(F32), 0.0)
    blocks = [u_ref[pl.ds(g, 16, stride=SUB), :] for g in range(SUB)]
    series = swap_blocks(blocks)
    for j in range(LANES):
        ri, beam = divmod(j, BEAMS)
        for i, m in enumerate(tiles):
            wide = jnp.concatenate([series[j][m : m + 1], series[j][m + 1 : m + 2]], axis=1)
            wide = jnp.broadcast_to(wide, (TAPS, 2 * TILE))
            turned = pltpu.roll(wide, 2 * TILE - (TAPS - 1), 1, stride=1, stride_axis=0)
            win_ref[beam, pl.ds(ri * TAPS, TAPS), pl.ds(i * TILE, TILE)] = turned[:, :TILE].astype(BF16)
    row = lax.broadcasted_iota(jnp.int32, (TAPS, TAPS), 0)
    col = lax.broadcasted_iota(jnp.int32, (TAPS, TAPS), 1)
    flip = jnp.where(row + col == TAPS - 1, 1.0, 0.0).astype(BF16)
    h_re = jnp.dot(h_ref[0], flip, preferred_element_type=F32)
    h_im = jnp.dot(h_ref[1], flip, preferred_element_type=F32)
    weights = jnp.concatenate(
        [jnp.concatenate([h_re, -h_im], axis=1), jnp.concatenate([h_im, h_re], axis=1)], axis=0
    ).astype(BF16)
    size = TEMPLATES * BEAMS
    for beam in range(BEAMS):
        resp = jnp.dot(weights, win_ref[beam], preferred_element_type=F32)
        re = resp[:TEMPLATES]
        im = resp[TEMPLATES:]
        power = re * re + im * im
        for i in range(len(tiles)):
            pow_ref[pl.ds(i * size + beam, TEMPLATES, stride=BEAMS), :] = power[:, i * TILE : (i + 1) * TILE]
    copies = []
    for i, m in enumerate(tiles):
        part = pow_ref[pl.ds(i * size, size), :]
        part_ref[i] = part.reshape(TEMPLATES, BEAMS, TILE).astype(BF16)
        copies.append(
            pltpu.make_async_copy(
                part_ref.at[i], out_ref.at[0, :, :, pl.ds(m * TILE, TILE)], sems.at[i]
            )
        )
        copies[-1].start()
    for copy in copies:
        copy.wait()


def response(place, y, templates, tiles, edges=(), before=()):
    width = y.shape[0] * GROUP
    count = len(tiles)
    vmem = pl.BlockSpec(memory_space=pltpu.VMEM)
    hbm = pl.BlockSpec(memory_space=pl.ANY)
    inputs = [near(y), *map(near, edges), templates]
    return pl.pallas_call(
        partial(response_kernel, tiles=tiles, edges=len(edges) > 0),
        grid_spec=pltpu.PrefetchScalarGridSpec(
            num_scalar_prefetch=1,
            in_specs=[vmem] * len(inputs) + [hbm] * len(before),
            out_specs=hbm,
            scratch_shapes=[
                pltpu.VMEM((16 * SUB, TILE), F32),
                pltpu.VMEM((BEAMS, 2 * TAPS, count * TILE), BF16),
                pltpu.VMEM((TEMPLATES * BEAMS * count, TILE), F32),
                pltpu.VMEM((count, TEMPLATES, BEAMS, TILE), BF16),
                pltpu.SemaphoreType.DMA((count,)),
            ],
        ),
        out_shape=jax.ShapeDtypeStruct((1, TEMPLATES, BEAMS, width), BF16),
        input_output_aliases={1 + len(inputs): 0} if before else {},
        compiler_params=pltpu.CompilerParams(vmem_limit_bytes=24 * 2**20),
        name="response",
    )(place, *inputs, *before)


def shards(spectra, delays, templates):
    width = spectra.shape[3]
    bins = lax.axis_size("bin")
    chans = lax.axis_size("chan")
    dms = lax.axis_size("dm")
    period = 2 * width * bins
    scale = 1.0 / math.sqrt(spectra.shape[2] * chans * dms)
    cores = PER_HOP // 8
    hops = chans // cores
    place = jnp.stack(
        [
            lax.axis_index("bin") * width,
            lax.axis_index("chan") // cores,
            bins - 1 - lax.axis_index("bin"),
            lax.axis_index("chan") % cores,
        ]
    ).astype(jnp.int32)
    table = delays.T

    def moved(x, s):
        return lax.ppermute(x, "chan", [(i, (i + s * cores) % chans) for i in range(chans)])

    other, weights, table = dedisperse(spectra, table, place, period, hops, True, BF16)
    other = lax.ppermute(
        other, "chan", [(i, i // cores * cores + cores - 1 - i % cores) for i in range(chans)]
    )
    (mine,) = dedisperse(weights, table, place, period, hops, False, F32)
    kept, *sent = join(mine, other)
    order = sorted(range(1, hops), key=lambda s: -min(s, hops - s))
    received = [moved(sent[s - 1], s) for s in order]
    received = lax.all_to_all(fold(kept, received), "dm", 0, 0, tiled=True)
    edge = TAPS // 2 // GROUP
    y, head, tail = finish(received, scale, edge)
    left = lax.ppermute(tail, "bin", [(i, (i + 1) % bins) for i in range(bins)])
    right = lax.ppermute(head, "bin", [((i + 1) % bins, i) for i in range(bins)])
    tiles = tuple(range(width // TILE))
    inner = response(place, y, templates, tiles[1:-1])
    return response(place, y, templates, (tiles[0], tiles[-1]), (left, right), (inner,))


def solution(mesh):
    placed = (P(None, None, ("chan", "dm"), "bin"), P(("chan", "dm"), None), P())
    return jax.shard_map(
        shards,
        mesh=mesh,
        in_specs=placed,
        out_specs=P(("chan", "dm"), None, None, "bin"),
        check_vma=False,
    )
```

```python
import math
from functools import partial

import jax
import jax.numpy as jnp
from jax import lax
from jax.experimental import pallas as pl
from jax.experimental.pallas import tpu as pltpu
from jax.sharding import PartitionSpec as P

D = 64
BEAMS = 4
TEMPLATES = 64
TAPS = 64
GROUP = 16
TILE = 128
SUB = TILE // GROUP
LANES = 2 * BEAMS
PER_HOP = 16
STEPS = 1
PIECES = 1
PHASE_DT = jnp.bfloat16
F32 = jnp.float32
BF16 = jnp.bfloat16


def swap_blocks(tiles):
    tiles = list(tiles)
    lane = lax.broadcasted_iota(jnp.int32, tiles[0].shape, 1)
    for step in (4, 2, 1):
        upper = (lane // GROUP) & step != 0
        fresh = list(tiles)
        for low in range(SUB):
            if low & step == 0:
                high = low | step
                fresh[low] = jnp.where(upper, pltpu.roll(tiles[high], step * GROUP, 1), tiles[low])
                fresh[high] = jnp.where(
                    upper, tiles[high], pltpu.roll(tiles[low], TILE - step * GROUP, 1)
                )
        tiles = fresh
    return tiles


def unit(count, period):
    quarter = period // 4
    rest = (count & (period - 1)) + quarter // 2
    turns = rest // quarter
    x = ((rest & (quarter - 1)) - quarter // 2).astype(F32) * (2.0 * math.pi / period)
    z = x * x
    sine = x * (1.0 + z * (-1.0 / 6 + z * (1.0 / 120 + z * (-1.0 / 5040 + z * (1.0 / 362880)))))
    cosine = 1.0 + z * (-0.5 + z * (1.0 / 24 + z * (-1.0 / 720 + z * (1.0 / 40320))))
    odd = turns & 1 == 1
    first = jnp.where(odd, sine, cosine)
    second = jnp.where(odd, cosine, sine)
    return (
        jnp.where((turns + 1) & 2 == 2, -first, first),
        jnp.where(turns & 2 == 2, -second, second),
    )


def times(a, b):
    return a[0] * b[0] - a[1] * b[1], a[0] * b[1] + a[1] * b[0]


def near(x):
    return pltpu.with_memory_space_constraint(x, pltpu.VMEM)


def far_away(x):
    return pltpu.with_memory_space_constraint(x, pltpu.HBM)


def channel_sums(place_ref, delay_ref, x_ref, *rest, period, hops, build, per_step):
    outs = 1
    out_refs, rest = rest[:outs], rest[outs:]
    if build:
        w_ref, copy_ref, fine_ref, mid_ref, base_ref, native_ref, sems = rest

        def fetch(t):
            part = native_ref.shape[3] // PIECES
            span = pl.ds(pl.multiple_of(t * part, TILE), part)
            return pltpu.make_async_copy(x_ref.at[:, :, :, span], native_ref.at[:, :, :, span], sems.at[t])

    else:
        w_ref = x_ref
        fine_ref, mid_ref, base_ref = rest
    step = pl.program_id(0)
    half = GROUP // 2
    count = hops * 8

    @pl.when(step == 0)
    def _():
        if build:
            for t in range(PIECES):
                fetch(t).start()
            copy_ref[...] = delay_ref[...]
        core = 1 - place_ref[3] if build else place_ref[3]
        first_rows = [(place_ref[1] + s) % hops * PER_HOP + core * 8 for s in range(hops)]
        n = jnp.concatenate([delay_ref[pl.ds(pl.multiple_of(r, 8), 8), :] for r in first_rows], axis=0)
        one = unit(n, period)
        group = unit(n * GROUP, period)
        wide = unit(n * TILE, period)
        start = unit(n * place_ref[0], period)
        power = one
        for j in range(1, half + 1):
            fine_ref[0, j] = power[0].astype(PHASE_DT)
            fine_ref[1, j] = power[1].astype(PHASE_DT)
            if j == half:
                mid = power
            power = times(power, one)
        for g in range(SUB):
            mid_ref[0, g] = mid[0]
            mid_ref[1, g] = mid[1]
            mid = times(mid, group)
        base_ref[0] = start[0]
        base_ref[1] = start[1]
        base_ref[2] = wide[0]
        base_ref[3] = wide[1]

    if build:
        lanes = lax.broadcasted_iota(jnp.int32, (128, TILE), 1)

    def build_weights(tile):
        span = pl.ds(pl.multiple_of(tile * TILE, TILE), TILE)
        native = [native_ref[j // BEAMS, j % BEAMS, :, span] for j in range(LANES)]
        for g, mixed in enumerate(swap_blocks(native)):
            at = tile * (SUB // 2) + g // 2
            w_ref[at, g % 2, 0:128] = mixed
            turned = pltpu.roll(mixed, TILE // 2, 1)
            w_ref[at, g % 2, 128:256] = jnp.where(lanes >= TILE // 2, -turned, turned)

    bin_of_lane = lax.broadcasted_iota(jnp.int32, (count, TILE), 1) & (GROUP - 1)

    def phases(base, g):
        turn = times(base, (mid_ref[0, g], mid_ref[1, g]))
        fc = turn[0].astype(PHASE_DT)
        fs = turn[1].astype(PHASE_DT)
        rows = [None] * GROUP
        rows[half] = (fc, fs)
        for j in range(1, half + 1):
            ec = fine_ref[0, j]
            es = fine_ref[1, j]
            cc = fc * ec
            ss = fs * es
            sc = fs * ec
            cs = fc * es
            if j < half:
                rows[half + j] = (cc - ss, sc + cs)
            rows[half - j] = (cc + ss, sc - cs)
        return [jnp.concatenate([c.astype(BF16), s.astype(BF16)], axis=1) for c, s in rows]

    def one_tile(tile, base):
        if build:
            build_weights(tile)
        for pair in range(SUB // 2):
            left = jnp.concatenate(phases(base, 2 * pair) + phases(base, 2 * pair + 1), axis=0)
            at = tile * (SUB // 2) + pair
            right = jnp.concatenate([w_ref[at, 0], w_ref[at, 1]], axis=1)
            prod = jnp.dot(left, right, preferred_element_type=F32)
            sides = []
            for side in range(2):
                cols = slice(side * TILE, (side + 1) * TILE)
                first = side * GROUP * count
                acc = prod[first : first + count, cols]
                for k in range(1, GROUP):
                    row = first + k * count
                    acc = jnp.where(bin_of_lane == k, prod[row : row + count, cols], acc)
                sides.append(acc.reshape(count // 8, 8, TILE))
            both = jnp.concatenate(sides, axis=1)
            part = both.shape[0] // outs
            at = pl.ds(pl.multiple_of(tile * SUB * 8 + pair * 16, 16), 16)
            for i, out_ref in enumerate(out_refs):
                out_ref[:, at, :] = both[i * part : (i + 1) * part].astype(out_ref.dtype)

    base = (base_ref[0], base_ref[1])
    wide = (base_ref[2], base_ref[3])
    per_piece = per_step * STEPS // PIECES
    for sub in range(per_step):
        if build and sub % per_piece == 0:
            fetch(step * (PIECES // STEPS) + sub // per_piece).wait()
        one_tile(step * per_step + sub, base)
        base = times(base, wide)
    base_ref[0] = base[0]
    base_ref[1] = base[1]


def dedisperse(x, delays, place, period, hops, build, dtype):
    tiles = x.shape[3] // TILE if build else x.shape[0] // (SUB // 2)
    count = hops * 8
    x_spec = pl.BlockSpec(memory_space=pl.ANY)
    stage = [pltpu.VMEM((2, BEAMS, 128, tiles * TILE), BF16), pltpu.SemaphoreType.DMA((PIECES,))]
    w_spec = pl.BlockSpec(memory_space=pltpu.VMEM)
    outs = 1
    part = count // 8 // outs
    out_specs = [pl.BlockSpec(memory_space=pltpu.VMEM)] * outs
    out_shapes = [pltpu.VMEM((part, tiles * SUB * 8, TILE), dtype)] * outs
    w_shape = pltpu.VMEM((tiles * SUB // 2, 2, 256, TILE), BF16)
    return pl.pallas_call(
        partial(channel_sums, period=period, hops=hops, build=build, per_step=tiles // STEPS),
        grid_spec=pltpu.PrefetchScalarGridSpec(
            num_scalar_prefetch=1,
            grid=(STEPS,),
            in_specs=[
                pl.BlockSpec((D, 128), lambda i, s: (0, 0)) if build else w_spec,
                x_spec if build else w_spec,
            ],
            out_specs=out_specs + [w_spec, w_spec] * build,
            scratch_shapes=[
                pltpu.VMEM((2, GROUP // 2 + 1, count, 128), PHASE_DT),
                pltpu.VMEM((2, SUB, count, 128), F32),
                pltpu.VMEM((4, count, 128), F32),
            ]
            + stage * build,
        ),
        out_shape=out_shapes + [w_shape, pltpu.VMEM(delays.shape, delays.dtype)] * build,
        compiler_params=pltpu.CompilerParams(vmem_limit_bytes=24 * 2**20),
        name="channel_sums",
    )(place, far_away(delays) if build else near(delays), far_away(x) if build else near(x))


def join_kernel(mine_ref, other_ref, keep_ref, *send_refs):
    keep_ref[...] = mine_ref[0] + other_ref[0].astype(F32)
    for s, send_ref in enumerate(send_refs, 1):
        send_ref[...] = (mine_ref[s] + other_ref[s].astype(F32)).astype(BF16)


def join(mine, other):
    vmem = pl.BlockSpec(memory_space=pltpu.VMEM)
    hops, rows, lanes = mine.shape
    return pl.pallas_call(
        join_kernel,
        in_specs=[vmem] * 2,
        out_specs=[vmem] * hops,
        out_shape=[pltpu.VMEM((rows, lanes), kind) for kind in [F32] + [BF16] * (hops - 1)],
        compiler_params=pltpu.CompilerParams(vmem_limit_bytes=24 * 2**20),
        name="join",
    )(near(mine), near(other))


def fold_kernel(keep_ref, *rest):
    *got_refs, out_ref, sum_ref = rest
    total = keep_ref[...]
    for ref in got_refs:
        total = total + ref[...].astype(F32)
    sum_ref[...] = total
    for d in range(8):
        out_ref[d] = sum_ref[pl.ds(d, total.shape[0] // 8, stride=8), :].astype(BF16)


def fold(kept, received):
    rows, lanes = kept.shape
    vmem = pl.BlockSpec(memory_space=pltpu.VMEM)
    return pl.pallas_call(
        fold_kernel,
        in_specs=[vmem] * (1 + len(received)),
        out_specs=vmem,
        out_shape=pltpu.VMEM((8, rows // 8, lanes), BF16),
        scratch_shapes=[pltpu.VMEM((rows, lanes), F32)],
        compiler_params=pltpu.CompilerParams(vmem_limit_bytes=24 * 2**20),
        name="fold",
    )(near(kept), *map(near, received))


def finish_kernel(x_ref, out_ref, head_ref, tail_ref, *, scale):
    total = x_ref[0].astype(F32)
    for i in range(1, x_ref.shape[0]):
        total = total + x_ref[i].astype(F32)
    y = (total * scale).astype(BF16)
    edge = head_ref.shape[0]
    out_ref[...] = y
    head_ref[...] = y[:edge]
    tail_ref[...] = y[y.shape[0] - edge :]


def finish(received, scale, edge):
    rows, lanes = received.shape[1:]
    return pl.pallas_call(
        partial(finish_kernel, scale=scale),
        in_specs=[pl.BlockSpec(memory_space=pltpu.VMEM)] * 1,
        out_specs=[pl.BlockSpec(memory_space=pltpu.VMEM)] * 3,
        out_shape=[pltpu.VMEM((n, lanes), BF16) for n in (rows, edge, edge)],
        compiler_params=pltpu.CompilerParams(vmem_limit_bytes=24 * 2**20),
        name="finish",
    )(near(received))


def response_kernel(place_ref, y_ref, *rest, tiles, edges):
    if edges:
        left_ref, right_ref, h_ref, _, out_ref, final_ref, u_ref, win_ref, pow_ref, sem = rest
    else:
        h_ref, out_ref, u_ref, win_ref, pow_ref = rest
    rows = y_ref.shape[0]
    edge = TAPS // 2 // GROUP
    u_ref[...] = jnp.zeros(u_ref.shape, F32)
    u_ref[pl.ds(edge, rows), :] = y_ref[...].astype(F32)
    if edges:
        u_ref[0:edge, :] = jnp.where(place_ref[0] > 0, left_ref[...].astype(F32), 0.0)
        u_ref[pl.ds(edge + rows, edge), :] = jnp.where(place_ref[2] > 0, right_ref[...].astype(F32), 0.0)
    blocks = [u_ref[pl.ds(g, 16, stride=SUB), :] for g in range(SUB)]
    series = swap_blocks(blocks)
    for j in range(LANES):
        ri, beam = divmod(j, BEAMS)
        for i, m in enumerate(tiles):
            wide = jnp.concatenate([series[j][m : m + 1], series[j][m + 1 : m + 2]], axis=1)
            wide = jnp.broadcast_to(wide, (TAPS, 2 * TILE))
            turned = pltpu.roll(wide, 2 * TILE - (TAPS - 1), 1, stride=1, stride_axis=0)
            win_ref[beam, pl.ds(ri * TAPS, TAPS), pl.ds(i * TILE, TILE)] = turned[:, :TILE].astype(BF16)
    row = lax.broadcasted_iota(jnp.int32, (TAPS, TAPS), 0)
    col = lax.broadcasted_iota(jnp.int32, (TAPS, TAPS), 1)
    flip = jnp.where(row + col == TAPS - 1, 1.0, 0.0).astype(BF16)
    h_re = jnp.dot(h_ref[0], flip, preferred_element_type=F32)
    h_im = jnp.dot(h_ref[1], flip, preferred_element_type=F32)
    weights = jnp.concatenate(
        [jnp.concatenate([h_re, -h_im], axis=1), jnp.concatenate([h_im, h_re], axis=1)], axis=0
    ).astype(BF16)
    size = TEMPLATES * BEAMS
    for beam in range(BEAMS):
        resp = jnp.dot(weights, win_ref[beam], preferred_element_type=F32)
        re = resp[:TEMPLATES]
        im = resp[TEMPLATES:]
        power = re * re + im * im
        for i in range(len(tiles)):
            pow_ref[pl.ds(i * size + beam, TEMPLATES, stride=BEAMS), :] = power[:, i * TILE : (i + 1) * TILE]
    for i, m in enumerate(tiles):
        part = pow_ref[pl.ds(i * size, size), :]
        out_ref[0, :, :, pl.ds(m * TILE, TILE)] = part.reshape(TEMPLATES, BEAMS, TILE).astype(BF16)
    if edges:
        copy = pltpu.make_async_copy(out_ref, final_ref, sem)
        copy.start()
        copy.wait()


def response(place, y, templates, tiles, edges=(), before=()):
    width = y.shape[0] * GROUP
    count = len(tiles)
    vmem = pl.BlockSpec(memory_space=pltpu.VMEM)
    hbm = pl.BlockSpec(memory_space=pl.ANY)
    shape = (1, TEMPLATES, BEAMS, width)
    inputs = [near(y), *map(near, edges), templates]
    return pl.pallas_call(
        partial(response_kernel, tiles=tiles, edges=len(edges) > 0),
        grid_spec=pltpu.PrefetchScalarGridSpec(
            num_scalar_prefetch=1,
            in_specs=[vmem] * (len(inputs) + len(before)),
            out_specs=[vmem] + [hbm] * len(before),
            scratch_shapes=[
                pltpu.VMEM((16 * SUB, TILE), F32),
                pltpu.VMEM((BEAMS, 2 * TAPS, count * TILE), BF16),
                pltpu.VMEM((TEMPLATES * BEAMS * count, TILE), F32),
            ]
            + [pltpu.SemaphoreType.DMA] * len(before),
        ),
        out_shape=[pltpu.VMEM(shape, BF16)] + [jax.ShapeDtypeStruct(shape, BF16)] * len(before),
        input_output_aliases={1 + len(inputs): 0} if before else {},
        compiler_params=pltpu.CompilerParams(vmem_limit_bytes=24 * 2**20),
        name="response",
    )(place, *inputs, *map(near, before))[-1]


def shards(spectra, delays, templates):
    width = spectra.shape[3]
    bins = lax.axis_size("bin")
    chans = lax.axis_size("chan")
    dms = lax.axis_size("dm")
    period = 2 * width * bins
    scale = 1.0 / math.sqrt(spectra.shape[2] * chans * dms)
    cores = PER_HOP // 8
    hops = chans // cores
    place = jnp.stack(
        [
            lax.axis_index("bin") * width,
            lax.axis_index("chan") // cores,
            bins - 1 - lax.axis_index("bin"),
            lax.axis_index("chan") % cores,
        ]
    ).astype(jnp.int32)
    table = delays.T

    def moved(x, s):
        return lax.ppermute(x, "chan", [(i, (i + s * cores) % chans) for i in range(chans)])

    other, weights, table = dedisperse(spectra, table, place, period, hops, True, BF16)
    other = lax.ppermute(
        other, "chan", [(i, i // cores * cores + cores - 1 - i % cores) for i in range(chans)]
    )
    (mine,) = dedisperse(weights, table, place, period, hops, False, F32)
    kept, *sent = join(mine, other)
    order = sorted(range(1, hops), key=lambda s: -min(s, hops - s))
    received = [moved(sent[s - 1], s) for s in order]
    received = lax.all_to_all(fold(kept, received), "dm", 0, 0, tiled=True)
    edge = TAPS // 2 // GROUP
    y, head, tail = finish(received, scale, edge)
    left = lax.ppermute(tail, "bin", [(i, (i + 1) % bins) for i in range(bins)])
    right = lax.ppermute(head, "bin", [((i + 1) % bins, i) for i in range(bins)])
    tiles = tuple(range(width // TILE))
    inner = response(place, y, templates, tiles[1:-1])
    return response(place, y, templates, (tiles[0], tiles[-1]), (left, right), (inner,))


def solution(mesh):
    placed = (P(None, None, ("chan", "dm"), "bin"), P(("chan", "dm"), None), P())
    return jax.shard_map(
        shards,
        mesh=mesh,
        in_specs=placed,
        out_specs=P(("chan", "dm"), None, None, "bin"),
        check_vma=False,
    )
```
